32 devices in a mesh: section: 2 (over y), expert: 16 (over z, x, core).
Axes of the slice: x: 2, y: 2, z: 4, core: 2. Of those that a mesh axis runs over, the one named last changes fastest.
Arguments:
- forward_input: bfloat16 [2, 2048, 2048], P('section', 'expert'), may hold values from -6 to 6
- forward_route: int32 [2, 2048, 1], P('section', 'expert'), may hold values from 0 to 3; in each aligned block of 128 rows (0 to 127, 128 to 255, ..., all dimensions but the last counted through in order) at most 40 rows name the same one
- forward_gates: float32 [2, 2048], P('section', 'expert'), may hold values from 0.25 to 1
- cotangent: bfloat16 [2, 2048, 2048], P('section', 'expert'), may hold values from -6 to 6
- backward_route: int32 [2, 2048, 1], P('section', 'expert'), may hold values from 0 to 3; in each aligned block of 128 rows (0 to 127, 128 to 255, ..., all dimensions but the last counted through in order) at most 40 rows name the same one
- backward_gates: float32 [2, 2048], P('section', 'expert'), may hold values from 0.25 to 1
- stash_held: bfloat16 [2, 16, 640, 384], P('section', 'expert'), may hold values from -6 to 6
- expert_in: bfloat16 [2, 16, 2048, 384], P('section', 'expert'), may hold values from -0.125 to 0.125
- expert_out: bfloat16 [2, 16, 192, 2048], P('section', 'expert'), may hold values from -0.21875 to 0.21875
Outputs:
- section_outputs: bfloat16 [2, 2048, 2048], P('section', 'expert')
- input_grads: bfloat16 [2, 2048, 2048], P('section', 'expert')
The draws below stay inside these ranges and needn't reach their ends.
Inputs may be any that keep to these rules, and one draw needn't show every extreme that they name: `forward_route`: in every aligned block of 128 tokens (the tokens of one index of expert) no expert is named by more than 40 tokens; 40 is reached in some blocks. `backward_route`: as for forward_route.
All inputs are finite; a program needn't handle non-finite values.
Results may differ from the reference program's by a relative error of at most 0.008.
Values may be sent and summed in bfloat16 or wider, within the bound.
A program may use at most 64 MiB of HBM per device.

```python
import math
import jax
import jax.numpy as jnp
import numpy as np
from jax import lax

D = 2048
HIDDEN_SIZE = 768
SPLIT = 4
TOK_DEV = 128
SECTIONS = 2
EXPERTS = 4
HID_DEV = 192
CAP = 40
ROWS = 640
TOKENS = 2048
N_EXPERT = 16


def levels(key, dims, pieces, smallest, high):
    factor_of = 1.0
    for dim, blocks in pieces:
        draws = jax.random.uniform(jax.random.fold_in(jax.random.fold_in(key, 6), dim), (blocks,), jnp.float32, smallest / len(pieces), high / len(pieces))
        factor_of = factor_of * jnp.repeat(jnp.exp(draws), dims[dim] // blocks).reshape((-1,) + (1,) * (len(dims) - 1 - dim))
    return factor_of


def assign_block(own_key, own, number, rows, count, top, most, skew):
    sequence = jax.random.permutation(own_key, count)
    packed, ordinary = portions_of(count, rows * top, most, skew, True), portions_of(count, rows * top, most, skew, False)
    places = jnp.arange(count)

    def named(sizes, rotation):
        used = int((sizes > 0).sum())
        fixed = max(1, used // 4)
        passed = fixed + (places - fixed + rotation * (used - fixed)) % max(1, count - fixed)
        return jnp.zeros((count,), jnp.int32).at[sequence[jnp.where(places < fixed, places, passed)]].set(jnp.asarray(sizes, jnp.int32))

    sizes = jnp.where(number % 4 == 0, named(packed, number // 4), named(ordinary, number - number // 4 - 1))
    mixed = jax.random.permutation(jax.random.fold_in(own, 3), count)
    source_of, sink = mixed[0:count // 2 * 2:2], mixed[1:count // 2 * 2:2]
    margin = jnp.minimum(sizes[source_of] - 1, most - sizes[sink]) // 2
    margin = jnp.where((source_of == sequence[0]) | (sink == sequence[0]) | (sizes[sink] == 0), 0, jnp.maximum(margin, 0))
    passed = jax.random.randint(jax.random.fold_in(own, 4), (count // 2,), 0, 1 << 20) % (margin + 1)
    sizes = sizes.at[source_of].add(-passed).at[sink].add(passed)
    members = jnp.searchsorted(jnp.cumsum(sizes), jnp.arange(rows * top), side="right").astype(jnp.int32)
    table = members.reshape(top, rows).T
    table = table[jax.random.permutation(jax.random.fold_in(own, 1), rows)]
    rotation = jax.random.randint(jax.random.fold_in(own, 2), (rows, 1), 0, top)
    return jnp.take_along_axis(table, (jnp.arange(top)[None, :] + rotation) % top, axis=1)


def portions_of(amount, total, limit, skew, full):
    portions = [(1 << 20) // math.isqrt(rank ** skew) + 1 for rank in range(1, amount + 1)]
    largest = limit if full else min(limit, max(-(-total // amount), total * portions[0] // sum(portions)))
    least = 1 if total - largest >= amount - 1 else 0
    counts, rest = [largest] + [least] * (amount - 1), total - largest - least * (amount - 1)
    while rest > 0:
        movable = [i for i in range(1, amount) if counts[i] < largest] or [i for i in range(1, amount) if counts[i] < limit]
        mass, left = sum([portions[i] for i in movable]), rest
        for i in movable:
            extra = min(limit - counts[i], max(1, left * portions[i] // mass), rest)
            counts[i] = counts[i] + extra
            rest = rest - extra
    return np.array(counts)


def gaussian(stream_key, shape, spread, most, split=(), kind=jnp.bfloat16):
    drawn = jax.random.normal(stream_key, shape, jnp.float32) * spread
    if len(split) > 0:
        drawn = levels(stream_key, shape, split, -0.22, 0.18) * drawn
    return jnp.clip(drawn, min=-most, max=most).astype(kind)


def setup_inputs(seed: int = 0) -> dict:
    streams_of = jax.random.split(jax.random.key(seed), 10)
    forward_input = gaussian(streams_of[0], (SECTIONS, TOKENS, D), 1.0, 6.0, ((0, 2), (1, 16)))
    forward_route_keys = jax.random.split(jax.random.fold_in(streams_of[1], 1), SECTIONS * TOKENS // TOK_DEV)
    forward_route_turns = jax.random.permutation(jax.random.fold_in(streams_of[1], 3), SECTIONS * TOKENS // TOK_DEV)
    forward_route = jax.vmap(lambda own, number: assign_block(jax.random.fold_in(streams_of[1], 2), own, number, TOK_DEV, EXPERTS, 1, CAP, 1))(forward_route_keys, forward_route_turns).reshape((SECTIONS, TOKENS, 1))
    forward_gates = jnp.clip(0.25 + 0.75 * jax.random.uniform(streams_of[2], (SECTIONS, TOKENS), jnp.float32) ** levels(streams_of[2], (SECTIONS, TOKENS), ((0, 2), (1, 16)), -0.2, 0.2), 0.25, 1.0)
    cotangent = gaussian(streams_of[3], (SECTIONS, TOKENS, D), 1.0, 6.0, ((0, 2), (1, 16)))
    backward_route_keys = jax.random.split(jax.random.fold_in(streams_of[4], 1), SECTIONS * TOKENS // TOK_DEV)
    backward_route_turns = jax.random.permutation(jax.random.fold_in(streams_of[4], 3), SECTIONS * TOKENS // TOK_DEV)
    backward_route = jax.vmap(lambda own, number: assign_block(jax.random.fold_in(streams_of[4], 2), own, number, TOK_DEV, EXPERTS, 1, CAP, 1))(backward_route_keys, backward_route_turns).reshape((SECTIONS, TOKENS, 1))
    backward_gates = jnp.clip(0.25 + 0.75 * jax.random.uniform(streams_of[5], (SECTIONS, TOKENS), jnp.float32) ** levels(streams_of[5], (SECTIONS, TOKENS), ((0, 2), (1, 16)), -0.2, 0.2), 0.25, 1.0)
    stash_held = gaussian(streams_of[6], (SECTIONS, N_EXPERT, ROWS, 2 * HID_DEV), 1.0, 6.0, ((0, 2), (1, 16)))
    expert_in = gaussian(streams_of[7], (SECTIONS, N_EXPERT, D, 2 * HID_DEV), D ** -0.5, 0.125, ((0, 2), (1, 16)))
    expert_out = gaussian(streams_of[8], (SECTIONS, N_EXPERT, HID_DEV, D), HIDDEN_SIZE ** -0.5, 0.21875, ((0, 2), (1, 16)))
    return dict(forward_input=forward_input, forward_route=forward_route, forward_gates=forward_gates, cotangent=cotangent, backward_route=backward_route, backward_gates=backward_gates, stash_held=stash_held, expert_in=expert_in, expert_out=expert_out)


def slot_numbers(routing):
    onehot = (routing[:, None] == jnp.arange(EXPERTS, dtype=jnp.int32)[None, :]).astype(jnp.int32)
    blocks = onehot.reshape(N_EXPERT, TOK_DEV, EXPERTS)
    before = (jnp.cumsum(blocks, axis=1) - blocks).astype(jnp.int32)
    rank_in = jnp.sum(before * blocks, axis=2).reshape(TOKENS).astype(jnp.int32)
    source = (jnp.arange(TOKENS, dtype=jnp.int32) // TOK_DEV).astype(jnp.int32)
    return (source * CAP + rank_in).astype(jnp.int32)


def scatter_rows(rows, routing, slots):
    buffer = jnp.zeros((EXPERTS, ROWS, D), rows.dtype)
    return buffer.at[routing, slots].set(rows)


def section_step(operands):
    inputs, route_fwd, gates_fwd, grads_in, route_bwd, gates_bwd, saved_rows, weight_in, weight_out = operands
    weight_in4 = weight_in.reshape(EXPERTS, SPLIT, D, 2 * HID_DEV).astype(jnp.float32)
    weight_out4 = weight_out.reshape(EXPERTS, SPLIT, HID_DEV, D).astype(jnp.float32)
    slots_fwd = slot_numbers(route_fwd)
    dispatched = scatter_rows(inputs, route_fwd, slots_fwd).astype(jnp.float32)
    gate_up = jnp.einsum('grd,gkdh->gkrh', dispatched, weight_in4)
    hidden = (jax.nn.silu(gate_up[..., :HID_DEV]) * gate_up[..., HID_DEV:]).astype(jnp.bfloat16)
    partial_value = jnp.einsum('gkrh,gkhd->gkrd', hidden.astype(jnp.float32), weight_out4).astype(jnp.bfloat16)
    summed = jnp.sum(partial_value.astype(jnp.float32), axis=1)
    picked = summed[route_fwd, slots_fwd]
    outputs = (inputs.astype(jnp.float32) + gates_fwd[:, None] * picked).astype(jnp.bfloat16)

    slots_bwd = slot_numbers(route_bwd)
    grad_rows = scatter_rows(grads_in, route_bwd, slots_bwd).astype(jnp.float32)
    saved_float = saved_rows.reshape(EXPERTS, SPLIT, ROWS, 2 * HID_DEV).astype(jnp.float32)
    gate_part = saved_float[..., :HID_DEV]
    up_part = saved_float[..., HID_DEV:]
    hidden_grad = jnp.einsum('grd,gkhd->gkrh', grad_rows, weight_out4)
    sigmoid_gate = jax.nn.sigmoid(gate_part)
    pre_grad = jnp.concatenate(
        [hidden_grad * up_part * sigmoid_gate * (1.0 + gate_part * (1.0 - sigmoid_gate)),
         hidden_grad * gate_part * sigmoid_gate], axis=3).astype(jnp.bfloat16)
    input_part = jnp.einsum('gkrh,gkdh->gkrd', pre_grad.astype(jnp.float32), weight_in4).astype(jnp.bfloat16)
    grad_sum = jnp.sum(input_part.astype(jnp.float32), axis=1)
    grad_picked = grad_sum[route_bwd, slots_bwd]
    grads_out = (grads_in.astype(jnp.float32) + gates_bwd[:, None] * grad_picked).astype(jnp.bfloat16)
    return outputs, grads_out


def reference(forward_input, forward_route, forward_gates, cotangent, backward_route, backward_gates, stash_held, expert_in, expert_out):
    operands = (forward_input, forward_route[:, :, 0], forward_gates, cotangent, backward_route[:, :, 0],
                backward_gates, stash_held[::-1], expert_in, expert_out)
    outputs, grads_out = lax.map(section_step, operands)
    blank = jnp.zeros((1, TOKENS, D), jnp.bfloat16)
    section_outputs = jnp.concatenate([blank, outputs[:-1]], axis=0)
    input_grads = jnp.concatenate([grads_out[1:], blank], axis=0)
    return section_outputs, input_grads
```

```python
import functools

import jax
import jax.numpy as jnp
from jax import lax
from jax.experimental import pallas as pl
from jax.experimental.pallas import tpu as pltpu
from jax.sharding import PartitionSpec as P

SPLIT = 4
MESH = pl.DeviceIdType.MESH
NT = (((1,), (1,)), ((), ()))


def flipped(index, mask):
    bit = 1
    while bit <= mask:
        if mask & bit:
            index = index + bit - 2 * bit * ((index // bit) % 2)
        bit *= 2
    return index


def far_first(groups):
    half = groups // 2
    return sorted(range(1, groups), key=lambda j: (j < half, j)) + [0]


def kernel(
    sections,
    groups,
    fin_hbm,
    froute_ref,
    fgate_ref,
    cot_hbm,
    broute_ref,
    bgate_ref,
    stash_hbm,
    win_hbm,
    wout_hbm,
    out_ref,
    grad_ref,
    x_buf,
    y_buf,
    place_buf,
    send_buf,
    rows_buf,
    z_buf,
    h_send,
    h_buf,
    q_send,
    q_buf,
    part_buf,
    red_own,
    red_far,
    sx_buf,
    red_x,
    sz_buf,
    back_buf,
    stash_buf,
    win,
    wall,
    zo_sem,
    xo_sem,
    co_sem,
    cf_sem,
    wx_sem,
    wc_sem,
    wf_sem,
    hx_sem,
    qx_sem,
    ro_sem,
    rf_sem,
    rx_sem,
    zb_sem,
    stash_sem,
    y_sem,
    w_sem,
    x_sem,
):
    section = lax.axis_index("section")
    me = lax.axis_index("expert")
    group, piece = me // SPLIT, me % SPLIT
    tokens, width = x_buf.shape[1:]
    cap = send_buf.shape[2]
    chunks, hid = wall.shape[1], wall.shape[1] * wall.shape[2]
    last = section == sections - 1
    mirror = sections - 1 - section
    order = far_first(groups)
    bf16, f32 = jnp.bfloat16, jnp.float32

    def z_peer(j):
        return {"expert": flipped(group, j) * SPLIT + piece}

    def peer(mask):
        return {"expert": group * SPLIT + flipped(piece, mask)}

    def load(which):
        return pltpu.make_async_copy((fin_hbm, cot_hbm)[which], x_buf.at[which], x_sem.at[which])

    barrier = pltpu.get_barrier_semaphore()

    def greet(where):
        pl.semaphore_signal(barrier, inc=1, device_id=where, device_id_type=MESH)

    for j in order[:-1]:
        greet(z_peer(j))
    for mask in range(1, SPLIT):
        greet(peer(mask))
    greet({"section": mirror})

    @pl.when(section < sections - 1)
    def _():
        greet({"section": section + 1})

    @pl.when(section > 0)
    def _():
        greet({"section": section - 1})

    def remote(src, dst, sem, index, where):
        return pltpu.make_async_remote_copy(
            src_ref=src,
            dst_ref=dst,
            send_sem=sem.at[(0, *index)],
            recv_sem=sem.at[(1, *index)],
            device_id=where,
            device_id_type=MESH,
        )

    def z_out(which, j):
        dst = z_buf.at[j] if which else rows_buf.at[j, 0]
        return remote(send_buf.at[which, j], dst, zo_sem, (which, j), z_peer(j))

    def x_out(j):
        return remote(rows_buf.at[j, 0], rows_buf.at[j, 2], xo_sem, (j,), peer(2))

    def c_out(j):
        return remote(rows_buf.at[j, 0], rows_buf.at[j, 1], co_sem, (j,), peer(1))

    def c_far(j):
        return remote(rows_buf.at[j, 2], rows_buf.at[j, 3], cf_sem, (j,), peer(1))

    def w_x(n):
        return remote(wout_hbm.at[n], wall.at[2, n], wx_sem, (n,), peer(2))

    def w_core(n):
        return remote(wout_hbm.at[n], wall.at[1, n], wc_sem, (n,), peer(1))

    def w_far(n):
        return remote(wall.at[2, n], wall.at[3, n], wf_sem, (n,), peer(1))

    def h_out(j, mask):
        return remote(h_send.at[j, mask], h_buf.at[j, mask], hx_sem, (j, mask), peer(mask))

    def q_out(b, mask):
        return remote(q_send.at[b, mask], q_buf.at[b, mask], qx_sem, (b, mask), peer(mask))

    def r_own(j):
        return remote(part_buf.at[j, 1], red_own.at[j], ro_sem, (j,), peer(1))

    def r_far(j):
        return remote(part_buf.at[j, 3], red_far.at[j], rf_sem, (j,), peer(1))

    def r_x(j):
        return remote(sx_buf.at[j], red_x.at[j], rx_sem, (j,), peer(2))

    def z_back(which, j):
        return remote(sz_buf.at[which, j], back_buf.at[which, j], zb_sem, (which, j), z_peer(j))

    def stash_copy(n):
        return remote(stash_hbm.at[n], stash_buf.at[n], stash_sem, (n,), {"section": mirror})

    def hand_over(which):
        return remote(
            y_buf.at[which],
            (out_ref, grad_ref)[which],
            y_sem,
            (which,),
            {"section": section + 1 - 2 * which},
        )

    load(0).start()
    load(1).start()
    w_copies = [pltpu.make_async_copy(win_hbm, win, w_sem.at[0])]
    w_copies.append(pltpu.make_async_copy(wout_hbm, wall.at[0], w_sem.at[1]))
    for copy in w_copies:
        copy.start()

    def pack(which):
        route = (froute_ref, broute_ref)[which][...]
        lanes = max(8, groups)
        expert = lax.broadcasted_iota(jnp.int32, (lanes, tokens), 0)
        onehot = (expert == route).astype(f32)
        upper = lax.broadcasted_iota(jnp.int32, (tokens, tokens), 0) < lax.broadcasted_iota(
            jnp.int32, (tokens, tokens), 1
        )
        before = jnp.dot(onehot.astype(bf16), upper.astype(f32).astype(bf16), preferred_element_type=f32)
        rank = jnp.sum(before * onehot, axis=0, keepdims=True).astype(jnp.int32)
        position = jnp.bitwise_xor(route, group) * cap + rank
        slots = lax.broadcasted_iota(jnp.int32, (groups * cap, tokens), 0)
        place = (slots == position).astype(f32).astype(bf16)
        place_buf[which] = place
        load(which).wait()
        packed = jnp.dot(place, x_buf[which], preferred_element_type=f32)
        packed = packed.reshape(groups, cap, width).astype(bf16)
        for j in range(1, groups):
            send_buf[which, j] = packed[j]
        if which:
            z_buf[0] = packed[0]
        else:
            rows_buf[0, 0] = packed[0]

    def combine(which):
        eye = lax.broadcasted_iota(jnp.int32, (tokens, tokens), 0) == lax.broadcasted_iota(
            jnp.int32, (tokens, tokens), 1
        )
        gates = jnp.sum(jnp.where(eye, (fgate_ref, bgate_ref)[which][...], 0.0), axis=1, keepdims=True)
        for j in order[:-1]:
            z_back(which, j).wait_recv()
        picked = lax.dot_general(
            place_buf[which],
            back_buf[which].reshape(groups * cap, width),
            (((0,), (0,)), ((), ())),
            preferred_element_type=f32,
        )
        y_buf[which] = (x_buf[which].astype(f32) + gates * picked).astype(bf16)

        @pl.when(section != (sections - 1) * (1 - which))
        def _():
            hand_over(which).start()

    def give(which, j, value):
        if j == 0:
            back_buf[which, 0] = value.astype(bf16)
        else:
            sz_buf[which, j] = value.astype(bf16)
            z_back(which, j).start()

    def w_start():
        for n in range(chunks):
            w_x(n).start()
        for n in range(chunks):
            w_core(n).start()

    def w_relay(n):
        w_x(n).wait_recv()
        w_far(n).start()

    def w_ready():
        w_copies[1].wait()
        for n in range(chunks):
            w_core(n).wait_recv()
            w_far(n).wait_recv()

    def f_share(j):
        if j:
            z_out(0, j).wait_recv()
        x_out(j).start()
        c_out(j).start()

    def f_relay(j):
        x_out(j).wait_recv()
        c_far(j).start()

    def f_hidden(j):
        c_out(j).wait_recv()
        c_far(j).wait_recv()
        rows = rows_buf[j].reshape(SPLIT * cap, width)
        gate_up = jnp.dot(rows, win[...], preferred_element_type=f32)
        gate, up = gate_up[:, :hid], gate_up[:, hid:]
        hidden = (gate / (1.0 + jnp.exp(-gate)) * up).reshape(SPLIT, cap, hid).astype(bf16)
        h_buf[j, 0] = hidden[0]
        for mask in (2, 3, 1):
            h_send[j, mask] = hidden[mask]
            h_out(j, mask).start()

    def f_out(j):
        total = jnp.dot(h_buf[j, 0], wall[0].reshape(hid, width), preferred_element_type=f32)
        for mask in range(1, SPLIT):
            h_out(j, mask).wait_recv()
            total += jnp.dot(h_buf[j, mask], wall[mask].reshape(hid, width), preferred_element_type=f32)
        give(0, j, total)

    def b_first(b):
        for j in (2 * b, 2 * b + 1):
            if j:
                z_out(1, j).wait_recv()
        rows = z_buf[pl.ds(2 * b, 2)].reshape(2 * cap, width)
        for mask in (2, 3, 1, 0):
            grad = lax.dot_general(rows, wall[mask].reshape(hid, width), NT, preferred_element_type=f32)
            grad = grad.reshape(2, cap, hid).astype(bf16)
            if mask:
                q_send[b, mask] = grad
                q_out(b, mask).start()
            else:
                q_buf[b, 0] = grad

    def b_ready(b):
        for mask in range(1, SPLIT):
            q_out(b, mask).wait_recv()

    def b_second(j):
        stash_copy(flipped(group, j)).wait_recv()
        saved = jnp.concatenate(
            [stash_buf[flipped(group, j), flipped(piece, mask)].astype(f32) for mask in range(SPLIT)], axis=0
        )
        grad = jnp.concatenate([q_buf[j // 2, mask, j % 2].astype(f32) for mask in range(SPLIT)], axis=0)
        gate, up = saved[:, :hid], saved[:, hid:]
        sig = 1.0 / (1.0 + jnp.exp(-gate))
        pre = jnp.concatenate(
            [grad * up * sig * (1.0 + gate * (1.0 - sig)), grad * gate * sig], axis=1
        ).astype(bf16)
        part = lax.dot_general(pre, win[...], NT, preferred_element_type=f32)
        part_buf[j] = part.reshape(SPLIT, cap, width).astype(bf16)
        r_far(j).start()
        r_own(j).start()

    def b_half(j):
        r_far(j).wait_recv()
        sx_buf[j] = (part_buf[j, 2].astype(f32) + red_far[j].astype(f32)).astype(bf16)
        r_x(j).start()

    def b_whole(j):
        r_own(j).wait_recv()
        r_x(j).wait_recv()
        give(1, j, part_buf[j, 0].astype(f32) + red_own[j].astype(f32) + red_x[j].astype(f32))

    def begin(first):
        pack(first)
        ends = jnp.where(section == 0, 1, 0) + jnp.where(last, 1, 0)
        pl.semaphore_wait(barrier, groups + 5 - ends)
        w_start()
        for j in order[:-1]:
            z_out(first, j).start()
        pack(1 - first)
        for j in order[:-1]:
            z_out(1 - first, j).start()
        for j in order:
            stash_copy(flipped(group, j)).start()
        w_copies[0].wait()

    near, far = order[groups // 2 :], order[: groups // 2]

    @pl.when(section < sections - 1)
    def _():
        begin(0)
        for i, j in enumerate(far):
            f_share(j)
            if i < chunks:
                w_relay(i)
        for n in range(len(far), chunks):
            w_relay(n)
        for j in near[:-1]:
            f_share(j)
        for j in far:
            f_relay(j)
        for j in far:
            f_hidden(j)
        f_share(0)
        w_ready()
        for j in near[:-1]:
            f_relay(j)
        for j in far:
            f_out(j)
        for b in range(groups // 4, groups // 2):
            b_first(b)
        for j in near[:-1]:
            f_hidden(j)
        f_relay(0)
        for b in range(groups // 4, groups // 2):
            b_ready(b)
        for i, j in enumerate(far):
            b_second(j)
            if i:
                b_half(far[i - 1])
        for j in near[:-1]:
            f_out(j)
        b_half(far[-1])
        for b in range(groups // 4):
            b_first(b)
        f_hidden(0)
        for j in far:
            b_whole(j)
        f_out(0)
        for b in range(groups // 4):
            b_ready(b)
        for i, j in enumerate(near):
            b_second(j)
            if i:
                b_half(near[i - 1])
        b_half(near[-1])
        combine(0)
        for j in near:
            b_whole(j)
        combine(1)

    @pl.when(last)
    def _():
        begin(1)
        for n in range(chunks):
            w_relay(n)
        w_ready()
        for b in range(groups // 4, groups // 2):
            b_first(b)
        f_share(0)
        for b in range(groups // 4):
            b_first(b)
        f_relay(0)
        for b in range(groups // 4, groups // 2):
            b_ready(b)
        for i, j in enumerate(far):
            b_second(j)
            if i:
                b_half(far[i - 1])
        b_half(far[-1])
        f_hidden(0)
        for j in far:
            f_share(j)
        for j in far:
            b_whole(j)
        for b in range(groups // 4):
            b_ready(b)
        for i, j in enumerate(near):
            b_second(j)
            if i:
                b_half(near[i - 1])
        b_half(near[-1])
        for j in far:
            f_relay(j)
        for j in near[:-1]:
            f_share(j)
        for j in far:
            f_hidden(j)
        for j in far:
            f_out(j)
        for j in near:
            b_whole(j)
        for j in near[:-1]:
            f_relay(j)
        combine(1)
        for j in near[:-1]:
            f_hidden(j)
        for j in near:
            f_out(j)
        combine(0)

    for n in range(chunks):
        w_x(n).wait_send()
        w_core(n).wait_send()
        w_far(n).wait_send()
    for j in range(groups):
        for copy in (x_out(j), c_out(j), c_far(j), r_own(j), r_far(j), r_x(j), stash_copy(j)):
            copy.wait_send()
        for mask in range(1, SPLIT):
            h_out(j, mask).wait_send()
        if j:
            for which in range(2):
                z_out(which, j).wait_send()
                z_back(which, j).wait_send()
    for b in range(groups // 2):
        for mask in range(1, SPLIT):
            q_out(b, mask).wait_send()
    for which in range(2):

        @pl.when(section != (sections - 1) * (1 - which))
        def _(which=which):
            hand_over(which).wait_send()

        @pl.when(section != (sections - 1) * which)
        def _(which=which):
            hand_over(which).wait_recv()


def place_kernel(sections, chunks, out_in, grad_in, out_ref, grad_ref, buf, in_sem, out_sem):
    section = lax.axis_index("section")
    size = buf.shape[1] // chunks

    def pieces(which, ref, inward):
        rows = [pl.ds(n * size, size) for n in range(chunks)]
        if inward:
            return [
                pltpu.make_async_copy(ref.at[r], buf.at[which, r], in_sem.at[which, n]) for n, r in enumerate(rows)
            ]
        return [pltpu.make_async_copy(buf.at[which, r], ref.at[r], out_sem.at[which, n]) for n, r in enumerate(rows)]

    for which, source in enumerate((out_in, grad_in)):

        @pl.when(section != (sections - 1) * which)
        def _(which=which, source=source):
            for copy in pieces(which, source, True):
                copy.start()

    for which, target in enumerate((out_ref, grad_ref)):

        @pl.when(section == (sections - 1) * which)
        def _(which=which, target=target):
            buf[which] = jnp.zeros(buf.shape[1:], buf.dtype)
            for copy in pieces(which, target, False):
                copy.start()

    for which, (source, target) in enumerate(((out_in, out_ref), (grad_in, grad_ref))):

        @pl.when(section != (sections - 1) * which)
        def _(which=which, source=source, target=target):
            for inward, outward in zip(pieces(which, source, True), pieces(which, target, False)):
                inward.wait()
                outward.start()

    for which, target in enumerate((out_ref, grad_ref)):
        for copy in pieces(which, target, False):
            copy.wait()


def solution(mesh):
    sections, shards = mesh.shape["section"], mesh.shape["expert"]
    groups = shards // SPLIT

    def per_device(fin, froute, fgate, cot, broute, bgate, stash, w_in, w_out):
        tokens, width = fin.shape[1:]
        rows, hid2 = stash.shape[2:]
        slots = rows // shards
        cap = -(-slots // 8) * 8
        hid = w_out.shape[2]
        saved = stash.reshape(shards, slots, hid2)
        if cap != slots:
            saved = jnp.pad(saved, ((0, 0), (0, cap - slots), (0, 0)))
        saved = saved.reshape(groups, SPLIT, cap, hid2)
        parts = 2 if hid % 32 == 0 else 1
        bf16, dma = jnp.bfloat16, pltpu.SemaphoreType.DMA
        vmem, hbm = pl.BlockSpec(memory_space=pltpu.VMEM), pl.BlockSpec(memory_space=pl.ANY)
        shape = jax.ShapeDtypeStruct((tokens, width), bf16)
        outputs, grads = pl.pallas_call(
            functools.partial(kernel, sections, groups),
            out_shape=(shape, shape),
            in_specs=[hbm, vmem, vmem, hbm, vmem, vmem, hbm, hbm, hbm],
            out_specs=(hbm, hbm),
            scratch_shapes=[
                pltpu.VMEM((2, tokens, width), bf16),
                pltpu.VMEM((2, tokens, width), bf16),
                pltpu.VMEM((2, groups * cap, tokens), bf16),
                pltpu.VMEM((2, groups, cap, width), bf16),
                pltpu.VMEM((groups, SPLIT, cap, width), bf16),
                pltpu.VMEM((groups, cap, width), bf16),
                pltpu.VMEM((groups, SPLIT, cap, hid), bf16),
                pltpu.VMEM((groups, SPLIT, cap, hid), bf16),
                pltpu.VMEM((groups // 2, SPLIT, 2, cap, hid), bf16),
                pltpu.VMEM((groups // 2, SPLIT, 2, cap, hid), bf16),
                pltpu.VMEM((groups, SPLIT, cap, width), bf16),
                pltpu.VMEM((groups, cap, width), bf16),
                pltpu.VMEM((groups, cap, width), bf16),
                pltpu.VMEM((groups, cap, width), bf16),
                pltpu.VMEM((groups, cap, width), bf16),
                pltpu.VMEM((2, groups, cap, width), bf16),
                pltpu.VMEM((2, groups, cap, width), bf16),
                pltpu.VMEM((groups, SPLIT, cap, hid2), bf16),
                pltpu.VMEM((width, hid2), bf16),
                pltpu.VMEM((SPLIT, parts, hid // parts, width), bf16),
                dma((2, 2, groups)),
                dma((2, groups)),
                dma((2, groups)),
                dma((2, groups)),
                dma((2, parts)),
                dma((2, parts)),
                dma((2, parts)),
                dma((2, groups, SPLIT)),
                dma((2, groups // 2, SPLIT)),
                dma((2, groups)),
                dma((2, groups)),
                dma((2, groups)),
                dma((2, 2, groups)),
                dma((2, groups)),
                dma((2, 2)),
                dma((2,)),
                dma((2,)),
            ],
            compiler_params=pltpu.CompilerParams(
                collective_id=0, has_side_effects=True, vmem_limit_bytes=60 * 1024 * 1024
            ),
        )(
            fin[0],
            froute.reshape(1, tokens),
            fgate.reshape(1, tokens),
            cot[0],
            broute.reshape(1, tokens),
            bgate.reshape(1, tokens),
            saved,
            w_in[0, 0],
            w_out.reshape(parts, hid // parts, width),
        )
        chunks = 4
        outputs, grads = pl.pallas_call(
            functools.partial(place_kernel, sections, chunks),
            out_shape=(shape, shape),
            in_specs=[hbm, hbm],
            out_specs=(hbm, hbm),
            scratch_shapes=[
                pltpu.VMEM((2, tokens, width), bf16),
                pltpu.SemaphoreType.DMA((2, chunks)),
                pltpu.SemaphoreType.DMA((2, chunks)),
            ],
            compiler_params=pltpu.CompilerParams(vmem_limit_bytes=60 * 1024 * 1024),
        )(outputs, grads)
        return outputs[None], grads[None]

    three, four = P("section", "expert", None), P("section", "expert", None, None)
    two = P("section", "expert")
    return jax.shard_map(
        per_device,
        mesh=mesh,
        in_specs=(three, three, two, three, three, two, four, four, four),
        out_specs=(three, three),
        check_vma=False,
    )
```

```python
import functools

import jax
import jax.numpy as jnp
from jax import lax
from jax.experimental import pallas as pl
from jax.experimental.pallas import tpu as pltpu
from jax.sharding import PartitionSpec as P

SPLIT, HALVES = 4, 2
MESH = pl.DeviceIdType.MESH
NT = (((1,), (1,)), ((), ()))


def flipped(index, mask):
    bit = 1
    while bit <= mask:
        if mask & bit:
            index = index + bit - 2 * bit * ((index // bit) % 2)
        bit *= 2
    return index


def far_first(groups):
    half = groups // 2
    return sorted(range(1, groups), key=lambda j: (j < half, j)) + [0]


def kernel(
    sections,
    groups,
    fin_hbm,
    froute_ref,
    fgate_ref,
    cot_hbm,
    broute_ref,
    bgate_ref,
    stash_hbm,
    win_hbm,
    wout_hbm,
    out_ref,
    grad_ref,
    x_buf,
    y_buf,
    place_buf,
    send_buf,
    rows_buf,
    z_buf,
    h_send,
    h_buf,
    q_send,
    q_buf,
    pre_buf,
    part_buf,
    red_own,
    red_far,
    sx_buf,
    red_x,
    sz_buf,
    back_buf,
    stash_buf,
    win,
    wall,
    zo_sem,
    xo_sem,
    co_sem,
    cf_sem,
    wx_sem,
    wc_sem,
    wf_sem,
    hx_sem,
    qx_sem,
    ro_sem,
    rf_sem,
    rx_sem,
    zb_sem,
    stash_sem,
    y_sem,
    w_sem,
    x_sem,
):
    section = lax.axis_index("section")
    me = lax.axis_index("expert")
    group, piece = me // SPLIT, me % SPLIT
    tokens, width = x_buf.shape[1:]
    cap, side = send_buf.shape[2], width // HALVES
    chunks, hid = wall.shape[1], wall.shape[1] * wall.shape[2]
    last = section == sections - 1
    mirror = sections - 1 - section
    order, half = far_first(groups), groups // 2
    bf16, f32 = jnp.bfloat16, jnp.float32

    def z_peer(j):
        return {"expert": flipped(group, j) * SPLIT + piece}

    def peer(mask):
        return {"expert": group * SPLIT + flipped(piece, mask)}

    def load(which):
        return pltpu.make_async_copy((fin_hbm, cot_hbm)[which], x_buf.at[which], x_sem.at[which])

    barrier = pltpu.get_barrier_semaphore()

    def greet(where):
        pl.semaphore_signal(barrier, inc=1, device_id=where, device_id_type=MESH)

    for j in order[:-1]:
        greet(z_peer(j))
    for mask in range(1, SPLIT):
        greet(peer(mask))
    greet({"section": mirror})

    @pl.when(section < sections - 1)
    def _():
        greet({"section": section + 1})

    @pl.when(section > 0)
    def _():
        greet({"section": section - 1})

    def remote(src, dst, sem, index, where):
        return pltpu.make_async_remote_copy(
            src_ref=src,
            dst_ref=dst,
            send_sem=sem.at[(0, *index)],
            recv_sem=sem.at[(1, *index)],
            device_id=where,
            device_id_type=MESH,
        )

    def z_out(which, j):
        dst = z_buf.at[j] if which else rows_buf.at[j, 0]
        return remote(send_buf.at[which, j], dst, zo_sem, (which, j), z_peer(j))

    def x_out(j):
        return remote(rows_buf.at[j, 0], rows_buf.at[j, 2], xo_sem, (j,), peer(2))

    def c_out(j):
        return remote(rows_buf.at[j, 0], rows_buf.at[j, 1], co_sem, (j,), peer(1))

    def c_far(j):
        return remote(rows_buf.at[j, 2], rows_buf.at[j, 3], cf_sem, (j,), peer(1))

    def w_x(n):
        return remote(wall.at[0, n], wall.at[2, n], wx_sem, (n,), peer(2))

    def w_core(n):
        return remote(wall.at[0, n], wall.at[1, n], wc_sem, (n,), peer(1))

    def w_far(n):
        return remote(wall.at[2, n], wall.at[3, n], wf_sem, (n,), peer(1))

    def h_out(j, mask):
        return remote(h_send.at[j, mask], h_buf.at[j, mask], hx_sem, (j, mask), peer(mask))

    def q_out(mask):
        return remote(q_send.at[mask], q_buf.at[mask], qx_sem, (mask,), peer(mask))

    def r_own(j, h):
        return remote(part_buf.at[h, j, 1], red_own.at[h, j], ro_sem, (h, j), peer(1))

    def r_far(j, h):
        return remote(part_buf.at[h, j, 3], red_far.at[h, j], rf_sem, (h, j), peer(1))

    def r_x(j, h):
        return remote(sx_buf.at[h, j], red_x.at[h, j], rx_sem, (h, j), peer(2))

    def z_back(which, j, h):
        return remote(sz_buf.at[which, h, j], back_buf.at[which, h, j], zb_sem, (which, h, j), z_peer(j))

    def stash_copy(n):
        return remote(stash_hbm.at[n], stash_buf.at[n], stash_sem, (n,), {"section": mirror})

    def columns(h):
        return pl.ds(h * side, side)

    def hand_over(which, h):
        return remote(
            y_buf.at[which, h],
            (out_ref, grad_ref)[which].at[:, columns(h)],
            y_sem,
            (which, h),
            {"section": section + 1 - 2 * which},
        )

    load(0).start()
    load(1).start()
    w_copies = [pltpu.make_async_copy(win_hbm, win, w_sem.at[0])]
    w_copies.append(pltpu.make_async_copy(wout_hbm, wall.at[0], w_sem.at[1]))
    for copy in w_copies:
        copy.start()

    def pack(which):
        route = (froute_ref, broute_ref)[which][...]
        lanes = max(8, groups)
        expert = lax.broadcasted_iota(jnp.int32, (lanes, tokens), 0)
        onehot = (expert == route).astype(f32)
        upper = lax.broadcasted_iota(jnp.int32, (tokens, tokens), 0) < lax.broadcasted_iota(
            jnp.int32, (tokens, tokens), 1
        )
        before = jnp.dot(onehot.astype(bf16), upper.astype(f32).astype(bf16), preferred_element_type=f32)
        rank = jnp.sum(before * onehot, axis=0, keepdims=True).astype(jnp.int32)
        position = jnp.bitwise_xor(route, group) * cap + rank
        slots = lax.broadcasted_iota(jnp.int32, (groups * cap, tokens), 0)
        place = (slots == position).astype(f32).astype(bf16)
        place_buf[which] = place
        load(which).wait()
        packed = jnp.dot(place, x_buf[which], preferred_element_type=f32)
        packed = packed.reshape(groups, cap, width).astype(bf16)
        for j in range(1, groups):
            send_buf[which, j] = packed[j]
        if which:
            z_buf[0] = packed[0]
        else:
            rows_buf[0, 0] = packed[0]

    def combine(which, h):
        eye = lax.broadcasted_iota(jnp.int32, (tokens, tokens), 0) == lax.broadcasted_iota(
            jnp.int32, (tokens, tokens), 1
        )
        gates = jnp.sum(jnp.where(eye, (fgate_ref, bgate_ref)[which][...], 0.0), axis=1, keepdims=True)
        for j in order[:-1]:
            z_back(which, j, h).wait_recv()
        picked = lax.dot_general(
            place_buf[which],
            back_buf[which, h].reshape(groups * cap, side),
            (((0,), (0,)), ((), ())),
            preferred_element_type=f32,
        )
        y_buf[which, h] = (x_buf[which, :, columns(h)].astype(f32) + gates * picked).astype(bf16)

        @pl.when(section != (sections - 1) * (1 - which))
        def _():
            hand_over(which, h).start()

    def give(which, j, h, value):
        if j == 0:
            back_buf[which, h, 0] = value.astype(bf16)
        else:
            sz_buf[which, h, j] = value.astype(bf16)
            z_back(which, j, h).start()

    def w_start():
        w_copies[1].wait()
        for n in range(chunks):
            w_x(n).start()
        for n in range(chunks):
            w_core(n).start()

    def w_relay(n):
        w_x(n).wait_recv()
        w_far(n).start()

    def f_rows(j):
        z_out(0, j).wait_recv()

    def f_share(j):
        x_out(j).start()
        c_out(j).start()

    def f_relay(j):
        x_out(j).wait_recv()
        c_far(j).start()

    def f_hidden(j):
        c_out(j).wait_recv()
        c_far(j).wait_recv()
        rows = rows_buf[j].reshape(SPLIT * cap, width)
        gate_up = jnp.dot(rows, win[...], preferred_element_type=f32)
        gate, up = gate_up[:, :hid], gate_up[:, hid:]
        hidden = (gate / (1.0 + jnp.exp(-gate)) * up).reshape(SPLIT, cap, hid).astype(bf16)
        h_buf[j, 0] = hidden[0]
        for mask in (2, 3, 1):
            h_send[j, mask] = hidden[mask]
            h_out(j, mask).start()

    def w_core_ready():
        for n in range(chunks):
            w_core(n).wait_recv()

    def w_far_ready():
        for n in range(chunks):
            w_far(n).wait_recv()

    def f_out(j):
        total = jnp.dot(h_buf[j, 0], wall[0].reshape(hid, width), preferred_element_type=f32)
        for mask in range(1, SPLIT):
            h_out(j, mask).wait_recv()
            total += jnp.dot(h_buf[j, mask], wall[mask].reshape(hid, width), preferred_element_type=f32)
        for h in range(HALVES):
            give(0, j, h, total[:, h * side : (h + 1) * side])

    def b_rows():
        for j in order[:-1]:
            z_out(1, j).wait_recv()

    def b_first(*masks):
        rows = z_buf[...].reshape(groups * cap, width)
        for mask in masks:
            grad = lax.dot_general(rows, wall[mask].reshape(hid, width), NT, preferred_element_type=f32)
            grad = grad.reshape(groups, cap, hid).astype(bf16)
            if mask:
                q_send[mask] = grad
                q_out(mask).start()
            else:
                q_buf[0] = grad

    def b_ready():
        for mask in range(1, SPLIT):
            q_out(mask).wait_recv()

    def b_grad(j):
        stash_copy(flipped(group, j)).wait_recv()
        saved = jnp.concatenate(
            [stash_buf[flipped(group, j), flipped(piece, mask)].astype(f32) for mask in range(SPLIT)], axis=0
        )
        grad = jnp.concatenate([q_buf[mask, j].astype(f32) for mask in range(SPLIT)], axis=0)
        gate, up = saved[:, :hid], saved[:, hid:]
        sig = 1.0 / (1.0 + jnp.exp(-gate))
        pre_buf[j] = jnp.concatenate(
            [grad * up * sig * (1.0 + gate * (1.0 - sig)), grad * gate * sig], axis=1
        ).astype(bf16)

    def b_part(j, h):
        part = lax.dot_general(pre_buf[j], win[columns(h)], NT, preferred_element_type=f32)
        part_buf[h, j] = part.reshape(SPLIT, cap, side).astype(bf16)
        r_far(j, h).start()
        r_own(j, h).start()

    def b_half(j, h):
        r_far(j, h).wait_recv()
        sx_buf[h, j] = (part_buf[h, j, 2].astype(f32) + red_far[h, j].astype(f32)).astype(bf16)
        r_x(j, h).start()

    def b_whole(j, h):
        r_own(j, h).wait_recv()
        r_x(j, h).wait_recv()
        mine = part_buf[h, j, 0].astype(f32)
        give(1, j, h, mine + red_own[h, j].astype(f32) + red_x[h, j].astype(f32))

    outer = (group == 0) | (group == groups - 1)

    def outer_out(which):
        @pl.when(outer)
        def _():
            for j in order[half:-1] + order[:half]:
                z_out(which, j).start()

    def inner_out(which):
        @pl.when(jnp.logical_not(outer))
        def _():
            for j in order[:-1]:
                z_out(which, j).start()

    def begin(first):
        pack(first)
        ends = jnp.where(section == 0, 1, 0) + jnp.where(last, 1, 0)
        pl.semaphore_wait(barrier, groups + 5 - ends)
        w_start()
        outer_out(first)
        inner_out(first)
        pack(1 - first)
        outer_out(1 - first)
        for j in order:
            stash_copy(flipped(group, j)).start()
        w_copies[0].wait()

    far, mid = order[:half], order[half:-1]
    near = order[half:]

    @pl.when(section < sections - 1)
    def _():
        begin(0)
        for n in range(chunks // 2):
            w_relay(n)
        f_rows(far[0])
        f_share(far[0])
        for n in range(chunks // 2, chunks):
            w_relay(n)
            if n == chunks // 2:
                for j in far[1:]:
                    f_rows(j)
                    f_share(j)
                inner_out(1)
        w_core_ready()
        f_relay(far[0])
        w_far_ready()
        f_hidden(far[0])
        for j in mid:
            f_rows(j)
            f_share(j)
        for j in far[1:]:
            f_relay(j)
            f_hidden(j)
        f_out(far[0])
        f_share(0)
        for j in mid:
            f_relay(j)
        b_rows()
        b_first(2, 3, 1, 0)
        for j in far[1:]:
            f_out(j)
        for j in mid:
            f_hidden(j)
        f_relay(0)
        f_hidden(0)
        b_ready()
        for i, j in enumerate(far):
            b_grad(j)
            b_part(j, 0)
            b_part(j, 1)
            b_half(j, 0)
            b_half(j, 1)
        for j in mid:
            f_out(j)
        for j in near:
            b_grad(j)
            b_part(j, 0)
            b_part(j, 1)
            b_half(j, 0)
            b_half(j, 1)
        f_out(0)
        for j in far:
            b_whole(j, 0)
            b_whole(j, 1)
        combine(0, 0)
        combine(0, 1)
        for j in near:
            b_whole(j, 0)
            b_whole(j, 1)
        combine(1, 0)
        combine(1, 1)

    @pl.when(last)
    def _():
        begin(1)
        for n in range(chunks - 1):
            w_relay(n)
        w_core_ready()
        b_rows()
        inner_out(0)
        b_first(1, 0)
        w_relay(chunks - 1)
        b_first(2)
        w_far_ready()
        b_first(3)
        f_share(0)
        b_ready()
        b_grad(far[0])
        b_part(far[0], 0)
        b_half(far[0], 0)
        b_part(far[0], 1)
        f_rows(far[0])
        f_share(far[0])
        b_half(far[0], 1)
        for j in far[1:]:
            b_grad(j)
            b_part(j, 0)
            b_part(j, 1)
            b_half(j, 0)
            b_half(j, 1)
        for j in mid:
            b_grad(j)
            b_part(j, 0)
            b_part(j, 1)
        b_whole(far[0], 0)
        f_relay(far[0])
        f_hidden(far[0])
        for j in mid:
            b_half(j, 0)
            b_half(j, 1)
        b_whole(far[0], 1)
        for j in far[1:]:
            f_rows(j)
            f_share(j)
        b_grad(0)
        b_part(0, 0)
        b_part(0, 1)
        b_half(0, 0)
        for j in far[1:]:
            b_whole(j, 0)
            b_whole(j, 1)
        for j in mid:
            f_rows(j)
            f_share(j)
        for j in mid:
            b_whole(j, 0)
            b_whole(j, 1)
        f_out(far[0])
        for j in far[1:]:
            f_relay(j)
            f_hidden(j)
        b_half(0, 1)
        b_whole(0, 0)
        combine(1, 0)
        f_relay(0)
        f_hidden(0)
        for j in mid:
            f_relay(j)
            f_hidden(j)
        for j in far[1:]:
            f_out(j)
        b_whole(0, 1)
        combine(1, 1)
        for j in mid:
            f_out(j)
        f_out(0)
        combine(0, 0)
        combine(0, 1)

    for n in range(chunks):
        w_x(n).wait_send()
        w_core(n).wait_send()
        w_far(n).wait_send()
    for j in range(groups):
        for copy in (x_out(j), c_out(j), c_far(j), stash_copy(j)):
            copy.wait_send()
        for mask in range(1, SPLIT):
            h_out(j, mask).wait_send()
        for h in range(HALVES):
            for copy in (r_own(j, h), r_far(j, h), r_x(j, h)):
                copy.wait_send()
        if j:
            for which in range(2):
                z_out(which, j).wait_send()
                for h in range(HALVES):
                    z_back(which, j, h).wait_send()
    for mask in range(1, SPLIT):
        q_out(mask).wait_send()
    for which in range(2):

        @pl.when(section != (sections - 1) * (1 - which))
        def _(which=which):
            for h in range(HALVES):
                hand_over(which, h).wait_send()

        @pl.when(section != (sections - 1) * which)
        def _(which=which):
            for h in range(HALVES):
                hand_over(which, h).wait_recv()


def place_kernel(sections, chunks, out_in, grad_in, out_ref, grad_ref, buf, in_sem, out_sem):
    section = lax.axis_index("section")
    size = buf.shape[1] // chunks

    def pieces(which, ref, inward):
        rows = [pl.ds(n * size, size) for n in range(chunks)]
        if inward:
            return [
                pltpu.make_async_copy(ref.at[r], buf.at[which, r], in_sem.at[which, n]) for n, r in enumerate(rows)
            ]
        return [pltpu.make_async_copy(buf.at[which, r], ref.at[r], out_sem.at[which, n]) for n, r in enumerate(rows)]

    for which, source in enumerate((out_in, grad_in)):

        @pl.when(section != (sections - 1) * which)
        def _(which=which, source=source):
            for copy in pieces(which, source, True):
                copy.start()

    for which, target in enumerate((out_ref, grad_ref)):

        @pl.when(section == (sections - 1) * which)
        def _(which=which, target=target):
            buf[which] = jnp.zeros(buf.shape[1:], buf.dtype)
            for copy in pieces(which, target, False):
                copy.start()

    for which, (source, target) in enumerate(((out_in, out_ref), (grad_in, grad_ref))):

        @pl.when(section != (sections - 1) * which)
        def _(which=which, source=source, target=target):
            for inward, outward in zip(pieces(which, source, True), pieces(which, target, False)):
                inward.wait()
                outward.start()

    for which, target in enumerate((out_ref, grad_ref)):
        for copy in pieces(which, target, False):
            copy.wait()


def solution(mesh):
    sections, shards = mesh.shape["section"], mesh.shape["expert"]
    groups = shards // SPLIT

    def per_device(fin, froute, fgate, cot, broute, bgate, stash, w_in, w_out):
        tokens, width = fin.shape[1:]
        rows, hid2 = stash.shape[2:]
        slots = rows // shards
        cap = -(-slots // 8) * 8
        hid = w_out.shape[2]
        saved = stash.reshape(shards, slots, hid2)
        if cap != slots:
            saved = jnp.pad(saved, ((0, 0), (0, cap - slots), (0, 0)))
        saved = saved.reshape(groups, SPLIT, cap, hid2)
        parts = next(n for n in (4, 3, 2, 1) if hid % (16 * n) == 0)
        bf16, dma = jnp.bfloat16, pltpu.SemaphoreType.DMA
        vmem, hbm = pl.BlockSpec(memory_space=pltpu.VMEM), pl.BlockSpec(memory_space=pl.ANY)
        shape = jax.ShapeDtypeStruct((tokens, width), bf16)
        outputs, grads = pl.pallas_call(
            functools.partial(kernel, sections, groups),
            out_shape=(shape, shape),
            in_specs=[hbm, vmem, vmem, hbm, vmem, vmem, hbm, hbm, hbm],
            out_specs=(hbm, hbm),
            scratch_shapes=[
                pltpu.VMEM((2, tokens, width), bf16),
                pltpu.VMEM((2, HALVES, tokens, width // HALVES), bf16),
                pltpu.VMEM((2, groups * cap, tokens), bf16),
                pltpu.VMEM((2, groups, cap, width), bf16),
                pltpu.VMEM((groups, SPLIT, cap, width), bf16),
                pltpu.VMEM((groups, cap, width), bf16),
                pltpu.VMEM((groups, SPLIT, cap, hid), bf16),
                pltpu.VMEM((groups, SPLIT, cap, hid), bf16),
                pltpu.VMEM((SPLIT, groups, cap, hid), bf16),
                pltpu.VMEM((SPLIT, groups, cap, hid), bf16),
                pltpu.VMEM((groups, SPLIT * cap, hid2), bf16),
                pltpu.VMEM((HALVES, groups, SPLIT, cap, width // HALVES), bf16),
                pltpu.VMEM((HALVES, groups, cap, width // HALVES), bf16),
                pltpu.VMEM((HALVES, groups, cap, width // HALVES), bf16),
                pltpu.VMEM((HALVES, groups, cap, width // HALVES), bf16),
                pltpu.VMEM((HALVES, groups, cap, width // HALVES), bf16),
                pltpu.VMEM((2, HALVES, groups, cap, width // HALVES), bf16),
                pltpu.VMEM((2, HALVES, groups, cap, width // HALVES), bf16),
                pltpu.VMEM((groups, SPLIT, cap, hid2), bf16),
                pltpu.VMEM((width, hid2), bf16),
                pltpu.VMEM((SPLIT, parts, hid // parts, width), bf16),
                dma((2, 2, groups)),
                dma((2, groups)),
                dma((2, groups)),
                dma((2, groups)),
                dma((2, parts)),
                dma((2, parts)),
                dma((2, parts)),
                dma((2, groups, SPLIT)),
                dma((2, SPLIT)),
                dma((2, HALVES, groups)),
                dma((2, HALVES, groups)),
                dma((2, HALVES, groups)),
                dma((2, 2, HALVES, groups)),
                dma((2, groups)),
                dma((2, 2, HALVES)),
                dma((2,)),
                dma((2,)),
            ],
            compiler_params=pltpu.CompilerParams(
                collective_id=0, has_side_effects=True, vmem_limit_bytes=60 * 1024 * 1024
            ),
        )(
            fin[0],
            froute.reshape(1, tokens),
            fgate.reshape(1, tokens),
            cot[0],
            broute.reshape(1, tokens),
            bgate.reshape(1, tokens),
            saved,
            w_in[0, 0],
            w_out.reshape(parts, hid // parts, width),
        )
        chunks = 4
        outputs, grads = pl.pallas_call(
            functools.partial(place_kernel, sections, chunks),
            out_shape=(shape, shape),
            in_specs=[hbm, hbm],
            out_specs=(hbm, hbm),
            scratch_shapes=[
                pltpu.VMEM((2, tokens, width), bf16),
                pltpu.SemaphoreType.DMA((2, chunks)),
                pltpu.SemaphoreType.DMA((2, chunks)),
            ],
            compiler_params=pltpu.CompilerParams(vmem_limit_bytes=60 * 1024 * 1024),
        )(outputs, grads)
        return outputs[None], grads[None]

    three, four = P("section", "expert", None), P("section", "expert", None, None)
    two = P("section", "expert")
    return jax.shard_map(
        per_device,
        mesh=mesh,
        in_specs=(three, three, two, three, three, two, four, four, four),
        out_specs=(three, three),
        check_vma=False,
    )
```

```python
import functools

import jax
import jax.numpy as jnp
from jax import lax
from jax.experimental import pallas as pl
from jax.experimental.pallas import tpu as pltpu
from jax.sharding import PartitionSpec as P

SPLIT, HALVES = 4, 2
MESH = pl.DeviceIdType.MESH
Z_OUT, X_OUT, C_OUT, C_FAR, W_X, W_CORE, W_FAR, H_OUT, Q_OUT, R_OWN, R_FAR, R_X, STASH, Z_BACK, HAND, KINDS = (
    *range(14),
    15,
    17,
)
NT = (((1,), (1,)), ((), ()))


def flipped(index, mask):
    bit = 1
    while bit <= mask:
        if mask & bit:
            index = index + bit - 2 * bit * ((index // bit) % 2)
        bit *= 2
    return index


def far_first(groups):
    half = groups // 2
    return sorted(range(1, groups), key=lambda j: (j < half, j)) + [0]


def kernel(
    sections,
    groups,
    fin_hbm,
    froute_hbm,
    fgate_hbm,
    cot_hbm,
    broute_hbm,
    bgate_hbm,
    stash_hbm,
    win_hbm,
    wout_hbm,
    out_ref,
    grad_ref,
    route_buf,
    gate_buf,
    x_buf,
    y_buf,
    place_buf,
    send_buf,
    rows_buf,
    z_buf,
    h_send,
    h_buf,
    q_send,
    q_buf,
    pre_buf,
    part_buf,
    red_buf,
    red_far,
    sx_buf,
    sz_buf,
    back_buf,
    stash_buf,
    win,
    wall,
    sent,
    zo_sem,
    zr_sem,
    xo_sem,
    c_sem,
    wx_sem,
    w_all_sem,
    hx_sem,
    qx_sem,
    rf_sem,
    rw_sem,
    zb_sem,
    stash_sem,
    y_sem,
    w_sem,
    x_sem,
):
    section = lax.axis_index("section")
    me = lax.axis_index("expert")
    group, piece = me // SPLIT, me % SPLIT
    tokens, width = x_buf.shape[1:]
    cap, side = send_buf.shape[2], width // HALVES
    chunks, hid = wall.shape[1], wall.shape[1] * wall.shape[2]
    last = section == sections - 1
    mirror = sections - 1 - section
    order, half = far_first(groups), groups // 2
    bf16, f32 = jnp.bfloat16, jnp.float32

    def z_peer(j):
        return {"expert": flipped(group, j) * SPLIT + piece}

    def peer(mask):
        return {"expert": group * SPLIT + flipped(piece, mask)}

    def load(which):
        return pltpu.make_async_copy((fin_hbm, cot_hbm)[which], x_buf.at[which], x_sem.at[which])

    small_copies = [
        pltpu.make_async_copy(source, buf.at[which], w_sem.at[2 + n])
        for n, (source, buf, which) in enumerate(
            (
                (froute_hbm, route_buf, 0),
                (broute_hbm, route_buf, 1),
                (fgate_hbm, gate_buf, 0),
                (bgate_hbm, gate_buf, 1),
            )
        )
    ]
    for copy in small_copies:
        copy.start()
    load(0).start()
    load(1).start()
    barrier = pltpu.get_barrier_semaphore()

    def greet(where):
        pl.semaphore_signal(barrier, inc=1, device_id=where, device_id_type=MESH)

    for j in order[:-1]:
        greet(z_peer(j))
    for mask in range(1, SPLIT):
        greet(peer(mask))
    greet({"section": mirror})

    @pl.when(section < sections - 1)
    def _():
        greet({"section": section + 1})

    @pl.when(section > 0)
    def _():
        greet({"section": section - 1})

    def remote(src, dst, kind, landed, where):
        return pltpu.make_async_remote_copy(
            src_ref=src,
            dst_ref=dst,
            send_sem=sent.at[kind],
            recv_sem=landed,
            device_id=where,
            device_id_type=MESH,
        )

    def await_bytes(ref, semaphore):
        pltpu.make_async_copy(ref, ref, semaphore).wait()

    def z_out(which, j):
        if which:
            return remote(send_buf.at[1, j], z_buf.at[j], Z_OUT, zr_sem.at[0], z_peer(j))
        return remote(send_buf.at[0, j], rows_buf.at[j, 0], Z_OUT, zo_sem.at[j], z_peer(j))

    def x_out(j):
        return remote(rows_buf.at[j, 0], rows_buf.at[j, 2], X_OUT, xo_sem.at[j], peer(2))

    def c_out(j):
        return remote(rows_buf.at[j, 0], rows_buf.at[j, 1], C_OUT, c_sem.at[j], peer(1))

    def c_far(j):
        return remote(rows_buf.at[j, 2], rows_buf.at[j, 3], C_FAR, c_sem.at[j], peer(1))

    def w_x(n):
        return remote(wall.at[0, n], wall.at[2, n], W_X, wx_sem.at[n], peer(2))

    def w_core(n):
        return remote(wall.at[0, n], wall.at[1, n], W_CORE, w_all_sem.at[0], peer(1))

    def w_far(n):
        return remote(wall.at[2, n], wall.at[3, n], W_FAR, w_all_sem.at[1], peer(1))

    def h_out(j, mask):
        return remote(h_send.at[j, mask], h_buf.at[j, mask], H_OUT, hx_sem.at[j], peer(mask))

    def q_out(mask):
        return remote(q_send.at[mask], q_buf.at[mask], Q_OUT, qx_sem.at[0], peer(mask))

    def r_own(j, h):
        return remote(part_buf.at[h, j, 1], red_buf.at[h, j, 0], R_OWN, rw_sem.at[h, j], peer(1))

    def r_far(j, h):
        return remote(part_buf.at[h, j, 3], red_far.at[h, j], R_FAR, rf_sem.at[h, j], peer(1))

    def r_x(j, h):
        return remote(sx_buf.at[h, j], red_buf.at[h, j, 1], R_X, rw_sem.at[h, j], peer(2))

    def z_back(which, j, h):
        return remote(
            sz_buf.at[which, h, j], back_buf.at[which, h, j], Z_BACK + which, zb_sem.at[which, h], z_peer(j)
        )

    def stash_copy(n):
        return remote(stash_hbm.at[n], stash_buf.at[n], STASH, stash_sem.at[0], {"section": mirror})

    def columns(h):
        return pl.ds(h * side, side)

    def hand_over(which, h):
        return remote(
            y_buf.at[which, h],
            (out_ref, grad_ref)[which].at[:, columns(h)],
            HAND + which,
            y_sem.at[which],
            {"section": section + 1 - 2 * which},
        )

    w_copies = [pltpu.make_async_copy(win_hbm, win, w_sem.at[0])]
    w_copies.append(pltpu.make_async_copy(wout_hbm, wall.at[0], w_sem.at[1]))
    for copy in w_copies:
        copy.start()

    def pack(which):
        small_copies[which].wait()
        route = route_buf[which]
        lanes = max(8, groups)
        expert = lax.broadcasted_iota(jnp.int32, (lanes, tokens), 0)
        onehot = (expert == route).astype(f32)
        upper = lax.broadcasted_iota(jnp.int32, (tokens, tokens), 0) < lax.broadcasted_iota(
            jnp.int32, (tokens, tokens), 1
        )
        before = jnp.dot(onehot.astype(bf16), upper.astype(f32).astype(bf16), preferred_element_type=f32)
        rank = jnp.sum(before * onehot, axis=0, keepdims=True).astype(jnp.int32)
        position = jnp.bitwise_xor(route, group) * cap + rank
        slots = lax.broadcasted_iota(jnp.int32, (groups * cap, tokens), 0)
        place = (slots == position).astype(f32).astype(bf16)
        place_buf[which] = place
        load(which).wait()
        packed = jnp.dot(place, x_buf[which], preferred_element_type=f32)
        packed = packed.reshape(groups, cap, width).astype(bf16)
        for j in range(1, groups):
            send_buf[which, j] = packed[j]
        if which:
            z_buf[0] = packed[0]
        else:
            rows_buf[0, 0] = packed[0]

    def combine(which, h):
        eye = lax.broadcasted_iota(jnp.int32, (tokens, tokens), 0) == lax.broadcasted_iota(
            jnp.int32, (tokens, tokens), 1
        )
        gates = jnp.sum(jnp.where(eye, gate_buf[which], 0.0), axis=1, keepdims=True)
        await_bytes(back_buf.at[which, h, pl.ds(1, groups - 1)], zb_sem.at[which, h])
        picked = lax.dot_general(
            place_buf[which],
            back_buf[which, h].reshape(groups * cap, side),
            (((0,), (0,)), ((), ())),
            preferred_element_type=f32,
        )
        y_buf[which, h] = (x_buf[which, :, columns(h)].astype(f32) + gates * picked).astype(bf16)

        @pl.when(section != (sections - 1) * (1 - which))
        def _():
            hand_over(which, h).start()

    def give(which, j, h, value):
        if j == 0:
            back_buf[which, h, 0] = value.astype(bf16)
        else:
            sz_buf[which, h, j] = value.astype(bf16)
            z_back(which, j, h).start()

    def w_start():
        w_copies[1].wait()
        for n in range(chunks):
            w_x(n).start()
        for n in range(chunks):
            w_core(n).start()

    def w_relay(n):
        w_x(n).wait_recv()
        w_far(n).start()

    def f_rows(j):
        z_out(0, j).wait_recv()

    def f_share(j):
        x_out(j).start()
        c_out(j).start()

    def f_relay(j):
        x_out(j).wait_recv()
        c_far(j).start()

    def f_hidden(j):
        await_bytes(rows_buf.at[j, pl.ds(1, 2)], c_sem.at[j])
        rows = rows_buf[j].reshape(SPLIT * cap, width)
        gate_up = jnp.dot(rows, win[...], preferred_element_type=f32)
        gate, up = gate_up[:, :hid], gate_up[:, hid:]
        hidden = (gate / (1.0 + jnp.exp(-gate)) * up).reshape(SPLIT, cap, hid).astype(bf16)
        h_buf[j, 0] = hidden[0]
        for mask in (2, 3, 1):
            h_send[j, mask] = hidden[mask]
            h_out(j, mask).start()

    def w_core_ready():
        await_bytes(wall.at[1], w_all_sem.at[0])

    def w_far_ready():
        await_bytes(wall.at[3], w_all_sem.at[1])

    def f_out(j):
        total = jnp.dot(h_buf[j, 0], wall[0].reshape(hid, width), preferred_element_type=f32)
        await_bytes(h_buf.at[j, pl.ds(1, SPLIT - 1)], hx_sem.at[j])
        for mask in range(1, SPLIT):
            total += jnp.dot(h_buf[j, mask], wall[mask].reshape(hid, width), preferred_element_type=f32)
        for h in range(HALVES):
            give(0, j, h, total[:, h * side : (h + 1) * side])

    def b_rows():
        await_bytes(z_buf.at[pl.ds(1, groups - 1)], zr_sem.at[0])

    def b_first(*masks):
        rows = z_buf[...].reshape(groups * cap, width)
        for mask in masks:
            grad = lax.dot_general(rows, wall[mask].reshape(hid, width), NT, preferred_element_type=f32)
            grad = grad.reshape(groups, cap, hid).astype(bf16)
            if mask:
                q_send[mask] = grad
                q_out(mask).start()
            else:
                q_buf[0] = grad

    def b_ready():
        await_bytes(q_buf.at[pl.ds(1, SPLIT - 1)], qx_sem.at[0])
        await_bytes(stash_buf, stash_sem.at[0])

    def b_grad(j):
        saved = jnp.concatenate(
            [stash_buf[flipped(group, j), flipped(piece, mask)].astype(f32) for mask in range(SPLIT)], axis=0
        )
        grad = jnp.concatenate([q_buf[mask, j].astype(f32) for mask in range(SPLIT)], axis=0)
        gate, up = saved[:, :hid], saved[:, hid:]
        sig = 1.0 / (1.0 + jnp.exp(-gate))
        pre_buf[j] = jnp.concatenate(
            [grad * up * sig * (1.0 + gate * (1.0 - sig)), grad * gate * sig], axis=1
        ).astype(bf16)

    def b_part(j, h):
        part = lax.dot_general(pre_buf[j], win[columns(h)], NT, preferred_element_type=f32)
        part_buf[h, j] = part.reshape(SPLIT, cap, side).astype(bf16)
        r_far(j, h).start()
        r_own(j, h).start()

    def b_half(j, h):
        r_far(j, h).wait_recv()
        sx_buf[h, j] = (part_buf[h, j, 2].astype(f32) + red_far[h, j].astype(f32)).astype(bf16)
        r_x(j, h).start()

    def b_whole(j, h):
        await_bytes(red_buf.at[h, j], rw_sem.at[h, j])
        mine = part_buf[h, j, 0].astype(f32)
        give(1, j, h, mine + red_buf[h, j, 0].astype(f32) + red_buf[h, j, 1].astype(f32))

    outer = (group == 0) | (group == groups - 1)

    def outer_out(which):
        @pl.when(outer)
        def _():
            for j in order[half:-1] + order[:half]:
                z_out(which, j).start()

    def inner_out(which):
        @pl.when(jnp.logical_not(outer))
        def _():
            for j in order[:-1]:
                z_out(which, j).start()

    def begin(first):
        pack(first)
        ends = jnp.where(section == 0, 1, 0) + jnp.where(last, 1, 0)
        pl.semaphore_wait(barrier, groups + 5 - ends)
        w_start()
        outer_out(first)
        inner_out(first)
        pack(1 - first)
        outer_out(1 - first)
        for j in order:
            stash_copy(flipped(group, j)).start()
        w_copies[0].wait()
        for copy in small_copies[2:]:
            copy.wait()

    def settle(which):
        for kind, ref in (
            (Z_OUT, send_buf.at[:, pl.ds(1, groups - 1)]),
            (X_OUT, rows_buf.at[:, 0]),
            (C_OUT, rows_buf.at[:, 0]),
            (C_FAR, rows_buf.at[:, 2]),
            (W_X, wall.at[0]),
            (W_CORE, wall.at[0]),
            (W_FAR, wall.at[2]),
            (H_OUT, h_send.at[:, pl.ds(1, SPLIT - 1)]),
            (Q_OUT, q_send.at[pl.ds(1, SPLIT - 1)]),
            (R_OWN, part_buf.at[:, :, 1]),
            (R_FAR, part_buf.at[:, :, 3]),
            (R_X, sx_buf),
            (STASH, stash_buf),
        ):
            await_bytes(ref, sent.at[kind])
        settle_last(which)

    def settle_last(which):
        await_bytes(sz_buf.at[which, :, pl.ds(1, groups - 1)], sent.at[Z_BACK + which])

    far, mid = order[:half], order[half:-1]
    near = order[half:]

    @pl.when(section < sections - 1)
    def _():
        begin(0)
        for n in range(chunks // 2):
            w_relay(n)
        f_rows(far[0])
        f_share(far[0])
        for n in range(chunks // 2, chunks):
            w_relay(n)
            if n == chunks // 2:
                for j in far[1:]:
                    f_rows(j)
                    f_share(j)
                inner_out(1)
        w_core_ready()
        f_relay(far[0])
        w_far_ready()
        f_hidden(far[0])
        for j in mid:
            f_rows(j)
            f_share(j)
        for j in far[1:]:
            f_relay(j)
            f_hidden(j)
        f_out(far[0])
        b_rows()
        b_first(2, 3, 1, 0)
        f_share(0)
        for j in mid:
            f_relay(j)
        for j in far[1:]:
            f_out(j)
        for j in mid:
            f_hidden(j)
        b_ready()
        for j in far:
            b_grad(j)
            b_part(j, 0)
            b_part(j, 1)
            b_half(j, 0)
            b_half(j, 1)
            if j == far[0]:
                f_relay(0)
        f_hidden(0)
        for j in mid:
            f_out(j)
        for j in mid:
            b_grad(j)
            b_part(j, 0)
            b_part(j, 1)
        b_whole(far[0], 0)
        for j in mid:
            b_half(j, 0)
        b_whole(far[0], 1)
        for j in mid:
            b_half(j, 1)
        b_grad(0)
        b_part(0, 0)
        b_part(0, 1)
        for j in far[1:]:
            b_whole(j, 0)
        b_half(0, 0)
        for j in far[1:]:
            b_whole(j, 1)
        b_half(0, 1)
        f_out(0)
        combine(0, 0)
        combine(0, 1)
        for j in mid:
            b_whole(j, 0)
            b_whole(j, 1)
        b_whole(0, 0)
        b_whole(0, 1)
        settle(0)
        combine(1, 0)
        combine(1, 1)
        settle_last(1)

    @pl.when(last)
    def _():
        begin(1)
        for n in range(chunks - 1):
            w_relay(n)
        w_core_ready()
        b_rows()
        inner_out(0)
        b_first(1, 0)
        w_relay(chunks - 1)
        b_first(2)
        w_far_ready()
        b_first(3)
        f_share(0)
        b_ready()
        b_grad(far[0])
        b_part(far[0], 0)
        b_half(far[0], 0)
        b_part(far[0], 1)
        f_rows(far[0])
        f_share(far[0])
        b_half(far[0], 1)
        for j in far[1:]:
            b_grad(j)
            b_part(j, 0)
            b_part(j, 1)
            b_half(j, 0)
            b_half(j, 1)
        f_relay(0)
        for j in mid:
            b_grad(j)
            b_part(j, 0)
            b_part(j, 1)
        b_whole(far[0], 0)
        f_relay(far[0])
        f_hidden(far[0])
        for j in mid:
            b_half(j, 0)
            b_half(j, 1)
        b_whole(far[0], 1)
        for j in far[1:]:
            f_rows(j)
            f_share(j)
        b_grad(0)
        b_part(0, 0)
        b_part(0, 1)
        b_half(0, 0)
        for j in far[1:]:
            b_whole(j, 0)
            b_whole(j, 1)
        for j in mid:
            f_rows(j)
            f_share(j)
        for j in mid:
            b_whole(j, 0)
            b_whole(j, 1)
        f_out(far[0])
        for j in far[1:]:
            f_relay(j)
            f_hidden(j)
        b_half(0, 1)
        b_whole(0, 0)
        combine(1, 0)
        f_hidden(0)
        for j in far[1:]:
            f_out(j)
        for j in mid:
            f_relay(j)
        b_whole(0, 1)
        combine(1, 1)
        for j in mid:
            f_hidden(j)
        for j in mid:
            f_out(j)
        f_out(0)
        settle(1)
        combine(0, 0)
        combine(0, 1)
        settle_last(0)

    for which in range(2):

        @pl.when(section != (sections - 1) * (1 - which))
        def _(which=which):
            await_bytes(y_buf.at[which], sent.at[HAND + which])

        @pl.when(section != (sections - 1) * which)
        def _(which=which):
            await_bytes((out_ref, grad_ref)[which], y_sem.at[which])


def place_kernel(sections, out_in, grad_in, out_ref, grad_ref, zeros, sem):
    section = lax.axis_index("section")

    def place(which, source):
        return pltpu.make_async_copy(source, (out_ref, grad_ref)[which], sem.at[which])

    for which, source in enumerate((out_in, grad_in)):

        @pl.when(section != (sections - 1) * which)
        def _(which=which, source=source):
            place(which, source).start()

        @pl.when(section == (sections - 1) * which)
        def _(which=which):
            zeros[...] = jnp.zeros(zeros.shape, zeros.dtype)
            place(which, zeros).start()

    for which in range(2):
        place(which, zeros).wait()


def solution(mesh):
    sections, shards = mesh.shape["section"], mesh.shape["expert"]
    groups = shards // SPLIT

    def per_device(fin, froute, fgate, cot, broute, bgate, stash, w_in, w_out):
        tokens, width = fin.shape[1:]
        rows, hid2 = stash.shape[2:]
        slots = rows // shards
        cap = -(-slots // 8) * 8
        hid = w_out.shape[2]
        saved = stash.reshape(shards, slots, hid2)
        if cap != slots:
            saved = jnp.pad(saved, ((0, 0), (0, cap - slots), (0, 0)))
        saved = saved.reshape(groups, SPLIT, cap, hid2)
        parts = next(n for n in (4, 3, 2, 1) if hid % (16 * n) == 0)
        bf16, dma = jnp.bfloat16, pltpu.SemaphoreType.DMA
        hbm = pl.BlockSpec(memory_space=pl.ANY)
        shape, held = jax.ShapeDtypeStruct((tokens, width), bf16), pltpu.VMEM((tokens, width), bf16)
        outputs, grads = pl.pallas_call(
            functools.partial(kernel, sections, groups),
            out_shape=(held, held),
            in_specs=[hbm] * 9,
            out_specs=(hbm, hbm),
            scratch_shapes=[
                pltpu.VMEM((2, 1, tokens), jnp.int32),
                pltpu.VMEM((2, 1, tokens), jnp.float32),
                pltpu.VMEM((2, tokens, width), bf16),
                pltpu.VMEM((2, HALVES, tokens, width // HALVES), bf16),
                pltpu.VMEM((2, groups * cap, tokens), bf16),
                pltpu.VMEM((2, groups, cap, width), bf16),
                pltpu.VMEM((groups, SPLIT, cap, width), bf16),
                pltpu.VMEM((groups, cap, width), bf16),
                pltpu.VMEM((groups, SPLIT, cap, hid), bf16),
                pltpu.VMEM((groups, SPLIT, cap, hid), bf16),
                pltpu.VMEM((SPLIT, groups, cap, hid), bf16),
                pltpu.VMEM((SPLIT, groups, cap, hid), bf16),
                pltpu.VMEM((groups, SPLIT * cap, hid2), bf16),
                pltpu.VMEM((HALVES, groups, SPLIT, cap, width // HALVES), bf16),
                pltpu.VMEM((HALVES, groups, 2, cap, width // HALVES), bf16),
                pltpu.VMEM((HALVES, groups, cap, width // HALVES), bf16),
                pltpu.VMEM((HALVES, groups, cap, width // HALVES), bf16),
                pltpu.VMEM((2, HALVES, groups, cap, width // HALVES), bf16),
                pltpu.VMEM((2, HALVES, groups, cap, width // HALVES), bf16),
                pltpu.VMEM((groups, SPLIT, cap, hid2), bf16),
                pltpu.VMEM((width, hid2), bf16),
                pltpu.VMEM((SPLIT, parts, hid // parts, width), bf16),
                dma((KINDS,)),
                dma((groups,)),
                dma((1,)),
                dma((groups,)),
                dma((groups,)),
                dma((parts,)),
                dma((2,)),
                dma((groups,)),
                dma((1,)),
                dma((HALVES, groups)),
                dma((HALVES, groups)),
                dma((2, HALVES)),
                dma((1,)),
                dma((2,)),
                dma((6,)),
                dma((2,)),
            ],
            compiler_params=pltpu.CompilerParams(
                collective_id=0, has_side_effects=True, vmem_limit_bytes=(64 * 1024 - 1280) * 1024
            ),
        )(
            fin[0],
            froute.reshape(1, tokens),
            fgate.reshape(1, tokens),
            cot[0],
            broute.reshape(1, tokens),
            bgate.reshape(1, tokens),
            saved,
            w_in[0, 0],
            w_out.reshape(parts, hid // parts, width),
        )
        outputs, grads = pl.pallas_call(
            functools.partial(place_kernel, sections),
            out_shape=(shape, shape),
            in_specs=[hbm, hbm],
            out_specs=(hbm, hbm),
            scratch_shapes=[pltpu.VMEM((tokens, width), bf16), dma((2,))],
            compiler_params=pltpu.CompilerParams(vmem_limit_bytes=8 * 1024 * 1024),
        )(outputs, grads)
        return outputs[None], grads[None]

    three, four = P("section", "expert", None), P("section", "expert", None, None)
    two = P("section", "expert")
    return jax.shard_map(
        per_device,
        mesh=mesh,
        in_specs=(three, three, two, three, three, two, four, four, four),
        out_specs=(three, three),
        check_vma=False,
    )
```

```python
import functools

import jax
import jax.numpy as jnp
from jax import lax
from jax.experimental import pallas as pl
from jax.experimental.pallas import tpu as pltpu
from jax.sharding import PartitionSpec as P

SPLIT, HALVES = 4, 2
MESH = pl.DeviceIdType.MESH
Z_OUT, X_OUT, C_OUT, C_FAR, W_X, W_CORE, W_FAR, H_OUT, Q_OUT, R_OWN, R_FAR, R_X, STASH, Z_BACK, HAND, KINDS = (
    *range(14),
    15,
    17,
)
NT = (((1,), (1,)), ((), ()))


def flipped(index, mask):
    bit = 1
    while bit <= mask:
        if mask & bit:
            index = index + bit - 2 * bit * ((index // bit) % 2)
        bit *= 2
    return index


def far_first(groups):
    half = groups // 2
    return sorted(range(1, groups), key=lambda j: (j < half, j)) + [0]


def kernel(
    sections,
    groups,
    fin_hbm,
    froute_hbm,
    fgate_hbm,
    cot_hbm,
    broute_hbm,
    bgate_hbm,
    stash_hbm,
    win_hbm,
    wout_hbm,
    out_ref,
    grad_ref,
    route_buf,
    gate_buf,
    x_buf,
    y_buf,
    place_buf,
    send_buf,
    rows_buf,
    z_buf,
    h_send,
    h_buf,
    q_send,
    q_buf,
    pre_buf,
    part_buf,
    red_buf,
    red_far,
    sx_buf,
    sz_buf,
    back_buf,
    stash_buf,
    win,
    wall,
    sent,
    zo_sem,
    zr_sem,
    xo_sem,
    c_sem,
    wx_sem,
    w_all_sem,
    hx_sem,
    qx_sem,
    rf_sem,
    rw_sem,
    zb_sem,
    stash_sem,
    y_sem,
    w_sem,
    x_sem,
):
    section = lax.axis_index("section")
    me = lax.axis_index("expert")
    group, piece = me // SPLIT, me % SPLIT
    tokens, width = x_buf.shape[1:]
    cap, side = send_buf.shape[2], width // HALVES
    chunks, hid = wall.shape[1], wall.shape[1] * wall.shape[2]
    lots = q_buf.shape[1]
    lot, strip = chunks // lots, hid // lots
    last = section == sections - 1
    mirror = sections - 1 - section
    order, half = far_first(groups), groups // 2
    bf16, f32 = jnp.bfloat16, jnp.float32

    def z_peer(j):
        return {"expert": flipped(group, j) * SPLIT + piece}

    def peer(mask):
        return {"expert": group * SPLIT + flipped(piece, mask)}

    def load(which):
        return pltpu.make_async_copy((fin_hbm, cot_hbm)[which], x_buf.at[which], x_sem.at[which])

    small_copies = [
        pltpu.make_async_copy(source, buf.at[which], w_sem.at[2 + n])
        for n, (source, buf, which) in enumerate(
            (
                (froute_hbm, route_buf, 0),
                (broute_hbm, route_buf, 1),
                (fgate_hbm, gate_buf, 0),
                (bgate_hbm, gate_buf, 1),
            )
        )
    ]
    for copy in small_copies:
        copy.start()
    load(0).start()
    load(1).start()
    barrier = pltpu.get_barrier_semaphore()

    def greet(where):
        pl.semaphore_signal(barrier, inc=1, device_id=where, device_id_type=MESH)

    for j in order[:-1]:
        greet(z_peer(j))
    for mask in range(1, SPLIT):
        greet(peer(mask))
    greet({"section": mirror})

    @pl.when(section < sections - 1)
    def _():
        greet({"section": section + 1})

    @pl.when(section > 0)
    def _():
        greet({"section": section - 1})

    def remote(src, dst, kind, landed, where):
        return pltpu.make_async_remote_copy(
            src_ref=src,
            dst_ref=dst,
            send_sem=sent.at[kind],
            recv_sem=landed,
            device_id=where,
            device_id_type=MESH,
        )

    def await_bytes(ref, semaphore):
        pltpu.make_async_copy(ref, ref, semaphore).wait()

    def z_out(which, j):
        if which:
            return remote(send_buf.at[1, j], z_buf.at[j], Z_OUT, zr_sem.at[0], z_peer(j))
        return remote(send_buf.at[0, j], rows_buf.at[j, 0], Z_OUT, zo_sem.at[j], z_peer(j))

    def x_out(j):
        return remote(rows_buf.at[j, 0], rows_buf.at[j, 2], X_OUT, xo_sem.at[j], peer(2))

    def c_out(j):
        return remote(rows_buf.at[j, 0], rows_buf.at[j, 1], C_OUT, c_sem.at[j], peer(1))

    def c_far(j):
        return remote(rows_buf.at[j, 2], rows_buf.at[j, 3], C_FAR, c_sem.at[j], peer(1))

    def w_x(n):
        return remote(wall.at[0, n], wall.at[2, n], W_X, wx_sem.at[n], peer(2))

    def w_core(n):
        return remote(wall.at[0, n], wall.at[1, n], W_CORE, w_all_sem.at[0], peer(1))

    def w_far(n):
        return remote(wall.at[2, n], wall.at[3, n], W_FAR, w_all_sem.at[1 + n // lot], peer(1))

    def h_out(j, mask):
        return remote(h_send.at[j, mask], h_buf.at[j, mask], H_OUT, hx_sem.at[j], peer(mask))

    def q_out(mask, c):
        return remote(q_send.at[mask, c], q_buf.at[mask, c], Q_OUT, qx_sem.at[0], peer(mask))

    def r_own(j, h):
        return remote(part_buf.at[h, j, 1], red_buf.at[h, j, 0], R_OWN, rw_sem.at[h, j], peer(1))

    def r_far(j, h):
        return remote(part_buf.at[h, j, 3], red_far.at[h, j], R_FAR, rf_sem.at[h, j], peer(1))

    def r_x(j, h):
        return remote(sx_buf.at[h, j], red_buf.at[h, j, 1], R_X, rw_sem.at[h, j], peer(2))

    def z_back(which, j, h):
        return remote(
            sz_buf.at[which, h, j], back_buf.at[which, h, j], Z_BACK + which, zb_sem.at[which, h], z_peer(j)
        )

    def stash_copy(n):
        return remote(stash_hbm.at[n], stash_buf.at[n], STASH, stash_sem.at[0], {"section": mirror})

    def columns(h):
        return pl.ds(h * side, side)

    def hand_over(which, h):
        return remote(
            y_buf.at[which, h],
            (out_ref, grad_ref)[which].at[:, columns(h)],
            HAND + which,
            y_sem.at[which],
            {"section": section + 1 - 2 * which},
        )

    w_copies = [pltpu.make_async_copy(win_hbm, win, w_sem.at[0])]
    w_copies.append(pltpu.make_async_copy(wout_hbm, wall.at[0], w_sem.at[1]))
    for copy in w_copies:
        copy.start()

    def pack(which):
        small_copies[which].wait()
        route = route_buf[which]
        lanes = max(8, groups)
        expert = lax.broadcasted_iota(jnp.int32, (lanes, tokens), 0)
        onehot = (expert == route).astype(f32)
        upper = lax.broadcasted_iota(jnp.int32, (tokens, tokens), 0) < lax.broadcasted_iota(
            jnp.int32, (tokens, tokens), 1
        )
        before = jnp.dot(onehot.astype(bf16), upper.astype(f32).astype(bf16), preferred_element_type=f32)
        rank = jnp.sum(before * onehot, axis=0, keepdims=True).astype(jnp.int32)
        position = jnp.bitwise_xor(route, group) * cap + rank
        slots = lax.broadcasted_iota(jnp.int32, (groups * cap, tokens), 0)
        place = (slots == position).astype(f32).astype(bf16)
        place_buf[which] = place
        load(which).wait()
        packed = jnp.dot(place, x_buf[which], preferred_element_type=f32)
        packed = packed.reshape(groups, cap, width).astype(bf16)
        for j in range(1, groups):
            send_buf[which, j] = packed[j]
        if which:
            z_buf[0] = packed[0]
        else:
            rows_buf[0, 0] = packed[0]

    def combine(which, h):
        eye = lax.broadcasted_iota(jnp.int32, (tokens, tokens), 0) == lax.broadcasted_iota(
            jnp.int32, (tokens, tokens), 1
        )
        gates = jnp.sum(jnp.where(eye, gate_buf[which], 0.0), axis=1, keepdims=True)
        await_bytes(back_buf.at[which, h, pl.ds(1, groups - 1)], zb_sem.at[which, h])
        picked = lax.dot_general(
            place_buf[which],
            back_buf[which, h].reshape(groups * cap, side),
            (((0,), (0,)), ((), ())),
            preferred_element_type=f32,
        )
        y_buf[which, h] = (x_buf[which, :, columns(h)].astype(f32) + gates * picked).astype(bf16)

        @pl.when(section != (sections - 1) * (1 - which))
        def _():
            hand_over(which, h).start()

    def give(which, j, h, value):
        if j == 0:
            back_buf[which, h, 0] = value.astype(bf16)
        else:
            sz_buf[which, h, j] = value.astype(bf16)
            z_back(which, j, h).start()

    def w_start():
        w_copies[1].wait()
        for n in range(chunks):
            w_x(n).start()
        for n in range(chunks):
            w_core(n).start()

    def w_relay(n):
        w_x(n).wait_recv()
        w_far(n).start()

    def f_rows(j):
        z_out(0, j).wait_recv()

    def f_share(j):
        x_out(j).start()
        c_out(j).start()

    def f_relay(j):
        x_out(j).wait_recv()
        c_far(j).start()

    def f_hidden(j):
        await_bytes(rows_buf.at[j, pl.ds(1, 2)], c_sem.at[j])
        rows = rows_buf[j].reshape(SPLIT * cap, width)
        gate_up = jnp.dot(rows, win[...], preferred_element_type=f32)
        gate, up = gate_up[:, :hid], gate_up[:, hid:]
        hidden = (gate / (1.0 + jnp.exp(-gate)) * up).reshape(SPLIT, cap, hid).astype(bf16)
        h_buf[j, 0] = hidden[0]
        for mask in (2, 3, 1):
            h_send[j, mask] = hidden[mask]
            h_out(j, mask).start()

    def w_core_ready():
        await_bytes(wall.at[1], w_all_sem.at[0])

    def w_far_ready(c):
        await_bytes(wall.at[3, pl.ds(c * lot, lot)], w_all_sem.at[1 + c])

    def f_out(j):
        total = jnp.dot(h_buf[j, 0], wall[0].reshape(hid, width), preferred_element_type=f32)
        await_bytes(h_buf.at[j, pl.ds(1, SPLIT - 1)], hx_sem.at[j])
        for mask in range(1, SPLIT):
            total += jnp.dot(h_buf[j, mask], wall[mask].reshape(hid, width), preferred_element_type=f32)
        for h in range(HALVES):
            give(0, j, h, total[:, h * side : (h + 1) * side])

    def b_rows():
        await_bytes(z_buf.at[pl.ds(1, groups - 1)], zr_sem.at[0])

    def b_give(mask, c, grad):
        grad = grad.reshape(groups, cap, strip).astype(bf16)
        if mask:
            q_send[mask, c] = grad
            q_out(mask, c).start()
        else:
            q_buf[0, c] = grad

    def b_first(*masks):
        rows = z_buf[...].reshape(groups * cap, width)
        for mask in masks:
            grad = lax.dot_general(rows, wall[mask].reshape(hid, width), NT, preferred_element_type=f32)
            for c in range(lots):
                b_give(mask, c, grad[:, c * strip : (c + 1) * strip])

    def b_lot(mask, c):
        rows = z_buf[...].reshape(groups * cap, width)
        weights = wall[mask, pl.ds(c * lot, lot)].reshape(strip, width)
        b_give(mask, c, lax.dot_general(rows, weights, NT, preferred_element_type=f32))

    def b_ready():
        await_bytes(q_buf.at[pl.ds(1, SPLIT - 1)], qx_sem.at[0])
        await_bytes(stash_buf, stash_sem.at[0])

    def b_grad(j):
        saved = jnp.concatenate(
            [stash_buf[flipped(group, j), flipped(piece, mask)].astype(f32) for mask in range(SPLIT)], axis=0
        )
        grad = jnp.concatenate(
            [
                jnp.concatenate([q_buf[mask, c, j].astype(f32) for mask in range(SPLIT)], axis=0)
                for c in range(lots)
            ],
            axis=1,
        )
        gate, up = saved[:, :hid], saved[:, hid:]
        sig = 1.0 / (1.0 + jnp.exp(-gate))
        pre_buf[j] = jnp.concatenate(
            [grad * up * sig * (1.0 + gate * (1.0 - sig)), grad * gate * sig], axis=1
        ).astype(bf16)

    def b_part(j, h):
        part = lax.dot_general(pre_buf[j], win[columns(h)], NT, preferred_element_type=f32)
        part_buf[h, j] = part.reshape(SPLIT, cap, side).astype(bf16)
        r_far(j, h).start()
        r_own(j, h).start()

    def b_half(j, h):
        r_far(j, h).wait_recv()
        sx_buf[h, j] = (part_buf[h, j, 2].astype(f32) + red_far[h, j].astype(f32)).astype(bf16)
        r_x(j, h).start()

    def b_whole(j, h):
        await_bytes(red_buf.at[h, j], rw_sem.at[h, j])
        mine = part_buf[h, j, 0].astype(f32)
        give(1, j, h, mine + red_buf[h, j, 0].astype(f32) + red_buf[h, j, 1].astype(f32))

    outer = (group == 0) | (group == groups - 1)

    def outer_out(which):
        @pl.when(outer)
        def _():
            for j in order[half:-1] + order[:half]:
                z_out(which, j).start()

    def inner_out(which):
        @pl.when(jnp.logical_not(outer))
        def _():
            for j in order[:-1]:
                z_out(which, j).start()

    def begin(first):
        pack(first)
        ends = jnp.where(section == 0, 1, 0) + jnp.where(last, 1, 0)
        pl.semaphore_wait(barrier, groups + 5 - ends)
        w_start()
        outer_out(first)
        inner_out(first)
        pack(1 - first)
        outer_out(1 - first)
        for j in order:
            stash_copy(flipped(group, j)).start()
        w_copies[0].wait()
        for copy in small_copies[2:]:
            copy.wait()

    def settle(which):
        for kind, ref in (
            (Z_OUT, send_buf.at[:, pl.ds(1, groups - 1)]),
            (X_OUT, rows_buf.at[:, 0]),
            (C_OUT, rows_buf.at[:, 0]),
            (C_FAR, rows_buf.at[:, 2]),
            (W_X, wall.at[0]),
            (W_CORE, wall.at[0]),
            (W_FAR, wall.at[2]),
            (H_OUT, h_send.at[:, pl.ds(1, SPLIT - 1)]),
            (Q_OUT, q_send.at[pl.ds(1, SPLIT - 1)]),
            (R_OWN, part_buf.at[:, :, 1]),
            (R_FAR, part_buf.at[:, :, 3]),
            (R_X, sx_buf),
            (STASH, stash_buf),
        ):
            await_bytes(ref, sent.at[kind])
        settle_last(which)

    def settle_last(which):
        await_bytes(sz_buf.at[which, :, pl.ds(1, groups - 1)], sent.at[Z_BACK + which])

    far, mid = order[:half], order[half:-1]
    near = order[half:]

    @pl.when(section < sections - 1)
    def _():
        begin(0)
        for n in range(chunks // 2):
            w_relay(n)
        f_rows(far[0])
        f_share(far[0])
        for n in range(chunks // 2, chunks):
            w_relay(n)
            if n == chunks // 2:
                for j in far[1:]:
                    f_rows(j)
                    f_share(j)
                inner_out(1)
        w_core_ready()
        f_relay(far[0])
        for c in range(lots):
            w_far_ready(c)
        f_hidden(far[0])
        for j in mid:
            f_rows(j)
            f_share(j)
        for j in far[1:]:
            f_relay(j)
            f_hidden(j)
        f_share(0)
        f_out(far[0])
        b_rows()
        b_first(2, 3, 1, 0)
        for j in mid:
            f_relay(j)
        for j in far[1:]:
            f_out(j)
        for j in mid:
            f_hidden(j)
        f_relay(0)
        b_ready()
        for j in far[:1]:
            b_grad(j)
            b_part(j, 0)
            b_part(j, 1)
        f_hidden(0)
        for j in far[:1]:
            b_half(j, 0)
            b_half(j, 1)
        for j in mid:
            f_out(j)
        for j in far[1:]:
            b_grad(j)
            b_part(j, 0)
            b_part(j, 1)
            b_half(j, 0)
            b_half(j, 1)
        f_out(0)
        for j in mid:
            b_grad(j)
            b_part(j, 0)
            b_part(j, 1)
        b_whole(far[0], 0)
        for j in mid:
            b_half(j, 0)
        b_whole(far[0], 1)
        for j in mid:
            b_half(j, 1)
        b_grad(0)
        b_part(0, 0)
        b_part(0, 1)
        for j in far[1:]:
            b_whole(j, 0)
        b_half(0, 0)
        combine(0, 0)
        combine(0, 1)
        for j in far[1:]:
            b_whole(j, 1)
        b_half(0, 1)
        for j in mid:
            b_whole(j, 0)
            b_whole(j, 1)
        b_whole(0, 0)
        b_whole(0, 1)
        settle(0)
        combine(1, 0)
        combine(1, 1)
        settle_last(1)

    @pl.when(last)
    def _():
        begin(1)
        for n in range(lot):
            w_relay(n)
        b_rows()
        inner_out(0)
        for n in range(lot, chunks - 1):
            w_relay(n)
        for c in range(lots - 1):
            b_lot(2, c)
            w_far_ready(c)
            b_lot(3, c)
        w_core_ready()
        b_first(1, 0)
        for n in range(max(lot, chunks - 1), chunks):
            w_relay(n)
        b_lot(2, lots - 1)
        w_far_ready(lots - 1)
        b_lot(3, lots - 1)
        f_share(0)
        b_ready()
        b_grad(far[0])
        b_part(far[0], 0)
        b_part(far[0], 1)
        for j in far[1:]:
            b_grad(j)
        b_half(far[0], 0)
        for j in far[1:]:
            b_part(j, 0)
        b_half(far[0], 1)
        for j in far[1:]:
            b_part(j, 1)
        f_rows(far[0])
        f_share(far[0])
        for j in far[1:]:
            b_half(j, 0)
            b_half(j, 1)
        f_relay(0)
        for j in mid:
            b_grad(j)
            b_part(j, 0)
            b_part(j, 1)
        for j in mid:
            b_half(j, 0)
        b_whole(far[0], 0)
        b_whole(far[0], 1)
        f_relay(far[0])
        f_hidden(far[0])
        for j in mid:
            b_half(j, 1)
        for j in far[1:]:
            f_rows(j)
            f_share(j)
        b_grad(0)
        b_part(0, 0)
        b_part(0, 1)
        b_half(0, 0)
        for j in far[1:]:
            b_whole(j, 0)
        for j in mid:
            f_rows(j)
            f_share(j)
        for j in mid:
            b_whole(j, 0)
        for j in far[1:]:
            b_whole(j, 1)
        for j in mid:
            b_whole(j, 1)
        f_out(far[0])
        for j in far[1:]:
            f_relay(j)
            f_hidden(j)
        b_half(0, 1)
        b_whole(0, 0)
        combine(1, 0)
        f_hidden(0)
        for j in mid:
            f_relay(j)
        for j in far[1:]:
            f_out(j)
        for j in mid:
            f_hidden(j)
        b_whole(0, 1)
        combine(1, 1)
        for j in mid:
            f_out(j)
        f_out(0)
        settle(1)
        combine(0, 0)
        combine(0, 1)
        settle_last(0)

    for which in range(2):

        @pl.when(section != (sections - 1) * (1 - which))
        def _(which=which):
            await_bytes(y_buf.at[which], sent.at[HAND + which])

        @pl.when(section != (sections - 1) * which)
        def _(which=which):
            await_bytes((out_ref, grad_ref)[which], y_sem.at[which])


def place_kernel(sections, out_in, grad_in, out_ref, grad_ref, zeros, sem):
    section = lax.axis_index("section")

    def place(which, source):
        return pltpu.make_async_copy(source, (out_ref, grad_ref)[which], sem.at[which])

    for which, source in enumerate((out_in, grad_in)):

        @pl.when(section != (sections - 1) * which)
        def _(which=which, source=source):
            place(which, source).start()

        @pl.when(section == (sections - 1) * which)
        def _(which=which):
            zeros[...] = jnp.zeros(zeros.shape, zeros.dtype)
            place(which, zeros).start()

    for which in range(2):
        place(which, zeros).wait()


def solution(mesh):
    sections, shards = mesh.shape["section"], mesh.shape["expert"]
    groups = shards // SPLIT

    def per_device(fin, froute, fgate, cot, broute, bgate, stash, w_in, w_out):
        tokens, width = fin.shape[1:]
        rows, hid2 = stash.shape[2:]
        slots = rows // shards
        cap = -(-slots // 8) * 8
        hid = w_out.shape[2]
        saved = stash.reshape(shards, slots, hid2)
        if cap != slots:
            saved = jnp.pad(saved, ((0, 0), (0, cap - slots), (0, 0)))
        saved = saved.reshape(groups, SPLIT, cap, hid2)
        parts = next(n for n in (4, 3, 2, 1) if hid % (16 * n) == 0)
        lots = 2 if parts % 2 == 0 else 1
        bf16, dma = jnp.bfloat16, pltpu.SemaphoreType.DMA
        hbm = pl.BlockSpec(memory_space=pl.ANY)
        shape, held = jax.ShapeDtypeStruct((tokens, width), bf16), pltpu.VMEM((tokens, width), bf16)
        outputs, grads = pl.pallas_call(
            functools.partial(kernel, sections, groups),
            out_shape=(held, held),
            in_specs=[hbm] * 9,
            out_specs=(hbm, hbm),
            scratch_shapes=[
                pltpu.VMEM((2, 1, tokens), jnp.int32),
                pltpu.VMEM((2, 1, tokens), jnp.float32),
                pltpu.VMEM((2, tokens, width), bf16),
                pltpu.VMEM((2, HALVES, tokens, width // HALVES), bf16),
                pltpu.VMEM((2, groups * cap, tokens), bf16),
                pltpu.VMEM((2, groups, cap, width), bf16),
                pltpu.VMEM((groups, SPLIT, cap, width), bf16),
                pltpu.VMEM((groups, cap, width), bf16),
                pltpu.VMEM((groups, SPLIT, cap, hid), bf16),
                pltpu.VMEM((groups, SPLIT, cap, hid), bf16),
                pltpu.VMEM((SPLIT, lots, groups, cap, hid // lots), bf16),
                pltpu.VMEM((SPLIT, lots, groups, cap, hid // lots), bf16),
                pltpu.VMEM((groups, SPLIT * cap, hid2), bf16),
                pltpu.VMEM((HALVES, groups, SPLIT, cap, width // HALVES), bf16),
                pltpu.VMEM((HALVES, groups, 2, cap, width // HALVES), bf16),
                pltpu.VMEM((HALVES, groups, cap, width // HALVES), bf16),
                pltpu.VMEM((HALVES, groups, cap, width // HALVES), bf16),
                pltpu.VMEM((2, HALVES, groups, cap, width // HALVES), bf16),
                pltpu.VMEM((2, HALVES, groups, cap, width // HALVES), bf16),
                pltpu.VMEM((groups, SPLIT, cap, hid2), bf16),
                pltpu.VMEM((width, hid2), bf16),
                pltpu.VMEM((SPLIT, parts, hid // parts, width), bf16),
                dma((KINDS,)),
                dma((groups,)),
                dma((1,)),
                dma((groups,)),
                dma((groups,)),
                dma((parts,)),
                dma((1 + lots,)),
                dma((groups,)),
                dma((1,)),
                dma((HALVES, groups)),
                dma((HALVES, groups)),
                dma((2, HALVES)),
                dma((1,)),
                dma((2,)),
                dma((6,)),
                dma((2,)),
            ],
            compiler_params=pltpu.CompilerParams(
                collective_id=0, has_side_effects=True, vmem_limit_bytes=(64 * 1024 - 1280) * 1024
            ),
        )(
            fin[0],
            froute.reshape(1, tokens),
            fgate.reshape(1, tokens),
            cot[0],
            broute.reshape(1, tokens),
            bgate.reshape(1, tokens),
            saved,
            w_in[0, 0],
            w_out.reshape(parts, hid // parts, width),
        )
        outputs, grads = pl.pallas_call(
            functools.partial(place_kernel, sections),
            out_shape=(shape, shape),
            in_specs=[hbm, hbm],
            out_specs=(hbm, hbm),
            scratch_shapes=[pltpu.VMEM((tokens, width), bf16), dma((2,))],
            compiler_params=pltpu.CompilerParams(vmem_limit_bytes=8 * 1024 * 1024),
        )(outputs, grads)
        return outputs[None], grads[None]

    three, four = P("section", "expert", None), P("section", "expert", None, None)
    two = P("section", "expert")
    return jax.shard_map(
        per_device,
        mesh=mesh,
        in_specs=(three, three, two, three, three, two, four, four, four),
        out_specs=(three, three),
        check_vma=False,
    )
```

```python
import functools

import jax
import jax.numpy as jnp
from jax import lax
from jax.experimental import pallas as pl
from jax.experimental.pallas import tpu as pltpu
from jax.sharding import PartitionSpec as P

SPLIT, HALVES = 4, 2
MESH = pl.DeviceIdType.MESH
Z_OUT, X_OUT, C_OUT, C_FAR, W_X, W_CORE, W_FAR, H_OUT, Q_OUT, R_OWN, R_FAR, R_X, STASH, Z_BACK, HAND, KINDS = (
    *range(14),
    15,
    17,
)
NT = (((1,), (1,)), ((), ()))


def flipped(index, mask):
    bit = 1
    while bit <= mask:
        if mask & bit:
            index = index + bit - 2 * bit * ((index // bit) % 2)
        bit *= 2
    return index


def far_first(groups):
    half = groups // 2
    return sorted(range(1, groups), key=lambda j: (j < half, j)) + [0]


def kernel(
    sections,
    groups,
    fin_hbm,
    froute_hbm,
    fgate_hbm,
    cot_hbm,
    broute_hbm,
    bgate_hbm,
    stash_hbm,
    win_hbm,
    wout_hbm,
    out_ref,
    grad_ref,
    route_buf,
    gate_buf,
    x_buf,
    y_buf,
    place_buf,
    send_buf,
    rows_buf,
    z_buf,
    h_send,
    h_buf,
    q_send,
    q_buf,
    pre_buf,
    part_buf,
    red_buf,
    red_far,
    sx_buf,
    sz_buf,
    back_buf,
    stash_buf,
    win,
    wall,
    sent,
    zo_sem,
    zr_sem,
    xo_sem,
    c_sem,
    wx_sem,
    w_all_sem,
    hx_sem,
    qx_sem,
    rf_sem,
    rw_sem,
    zb_sem,
    stash_sem,
    y_sem,
    w_sem,
    x_sem,
):
    section = lax.axis_index("section")
    me = lax.axis_index("expert")
    group, piece = me // SPLIT, me % SPLIT
    tokens, width = x_buf.shape[1:]
    cap, side = send_buf.shape[2], width // HALVES
    chunks, hid = wall.shape[1], wall.shape[1] * wall.shape[2]
    lots = q_buf.shape[1]
    lot, strip = chunks // lots, hid // lots
    last = section == sections - 1
    mirror = sections - 1 - section
    order, half = far_first(groups), groups // 2
    bf16, f32 = jnp.bfloat16, jnp.float32

    def z_peer(j):
        return {"expert": flipped(group, j) * SPLIT + piece}

    def peer(mask):
        return {"expert": group * SPLIT + flipped(piece, mask)}

    def load(which):
        return pltpu.make_async_copy((fin_hbm, cot_hbm)[which], x_buf.at[which], x_sem.at[which])

    small_copies = [
        pltpu.make_async_copy(source, buf.at[which], w_sem.at[2 + n])
        for n, (source, buf, which) in enumerate(
            (
                (froute_hbm, route_buf, 0),
                (broute_hbm, route_buf, 1),
                (fgate_hbm, gate_buf, 0),
                (bgate_hbm, gate_buf, 1),
            )
        )
    ]
    for copy in small_copies:
        copy.start()
    load(0).start()
    load(1).start()
    barrier = pltpu.get_barrier_semaphore()

    def greet(where):
        pl.semaphore_signal(barrier, inc=1, device_id=where, device_id_type=MESH)

    for j in order[:-1]:
        greet(z_peer(j))
    for mask in range(1, SPLIT):
        greet(peer(mask))
    greet({"section": mirror})

    @pl.when(section < sections - 1)
    def _():
        greet({"section": section + 1})

    @pl.when(section > 0)
    def _():
        greet({"section": section - 1})

    def remote(src, dst, kind, landed, where):
        return pltpu.make_async_remote_copy(
            src_ref=src,
            dst_ref=dst,
            send_sem=sent.at[kind],
            recv_sem=landed,
            device_id=where,
            device_id_type=MESH,
        )

    def await_bytes(ref, semaphore):
        pltpu.make_async_copy(ref, ref, semaphore).wait()

    def z_out(which, j):
        if which:
            return remote(send_buf.at[1, j], z_buf.at[j], Z_OUT, zr_sem.at[0], z_peer(j))
        return remote(send_buf.at[0, j], rows_buf.at[j, 0], Z_OUT, zo_sem.at[j], z_peer(j))

    def x_out(j):
        return remote(rows_buf.at[j, 0], rows_buf.at[j, 2], X_OUT, xo_sem.at[j], peer(2))

    def c_out(j):
        return remote(rows_buf.at[j, 0], rows_buf.at[j, 1], C_OUT, c_sem.at[j], peer(1))

    def c_far(j):
        return remote(rows_buf.at[j, 2], rows_buf.at[j, 3], C_FAR, c_sem.at[j], peer(1))

    def w_x(n):
        return remote(wall.at[0, n], wall.at[2, n], W_X, wx_sem.at[n], peer(2))

    def w_core(n):
        return remote(wall.at[0, n], wall.at[1, n], W_CORE, w_all_sem.at[0], peer(1))

    def w_far(n):
        return remote(wall.at[2, n], wall.at[3, n], W_FAR, w_all_sem.at[1 + n // lot], peer(1))

    def h_out(j, mask):
        return remote(h_send.at[j, mask], h_buf.at[j, mask], H_OUT, hx_sem.at[j], peer(mask))

    def q_out(mask, c):
        return remote(q_send.at[mask, c], q_buf.at[mask, c], Q_OUT, qx_sem.at[0], peer(mask))

    def r_own(j, h):
        return remote(part_buf.at[h, j, 1], red_buf.at[h, j, 0], R_OWN, rw_sem.at[h, j], peer(1))

    def r_far(j, h):
        return remote(part_buf.at[h, j, 3], red_far.at[h, j], R_FAR, rf_sem.at[h, j], peer(1))

    def r_x(j, h):
        return remote(sx_buf.at[h, j], red_buf.at[h, j, 1], R_X, rw_sem.at[h, j], peer(2))

    def z_back(which, j, h):
        return remote(
            sz_buf.at[which, h, j], back_buf.at[which, h, j], Z_BACK + which, zb_sem.at[which, h], z_peer(j)
        )

    def stash_copy(n):
        return remote(stash_hbm.at[n], stash_buf.at[n], STASH, stash_sem.at[0], {"section": mirror})

    def columns(h):
        return pl.ds(h * side, side)

    def hand_over(which, h):
        return remote(
            y_buf.at[which, h],
            (out_ref, grad_ref)[which].at[:, columns(h)],
            HAND + which,
            y_sem.at[which],
            {"section": section + 1 - 2 * which},
        )

    w_copies = [pltpu.make_async_copy(win_hbm, win, w_sem.at[0])]
    w_copies.append(pltpu.make_async_copy(wout_hbm, wall.at[0], w_sem.at[1]))
    for copy in w_copies:
        copy.start()

    def pack(which):
        small_copies[which].wait()
        route = route_buf[which]
        lanes = max(8, groups)
        expert = lax.broadcasted_iota(jnp.int32, (lanes, tokens), 0)
        onehot = (expert == route).astype(f32)
        upper = lax.broadcasted_iota(jnp.int32, (tokens, tokens), 0) < lax.broadcasted_iota(
            jnp.int32, (tokens, tokens), 1
        )
        before = jnp.dot(onehot.astype(bf16), upper.astype(f32).astype(bf16), preferred_element_type=f32)
        rank = jnp.sum(before * onehot, axis=0, keepdims=True).astype(jnp.int32)
        position = jnp.bitwise_xor(route, group) * cap + rank
        slots = lax.broadcasted_iota(jnp.int32, (groups * cap, tokens), 0)
        place = (slots == position).astype(f32).astype(bf16)
        place_buf[which] = place
        load(which).wait()
        packed = jnp.dot(place, x_buf[which], preferred_element_type=f32)
        packed = packed.reshape(groups, cap, width).astype(bf16)
        for j in range(1, groups):
            send_buf[which, j] = packed[j]
        if which:
            z_buf[0] = packed[0]
        else:
            rows_buf[0, 0] = packed[0]

    def combine(which, h):
        eye = lax.broadcasted_iota(jnp.int32, (tokens, tokens), 0) == lax.broadcasted_iota(
            jnp.int32, (tokens, tokens), 1
        )
        gates = jnp.sum(jnp.where(eye, gate_buf[which], 0.0), axis=1, keepdims=True)
        await_bytes(back_buf.at[which, h, pl.ds(1, groups - 1)], zb_sem.at[which, h])
        picked = lax.dot_general(
            place_buf[which],
            back_buf[which, h].reshape(groups * cap, side),
            (((0,), (0,)), ((), ())),
            preferred_element_type=f32,
        )
        y_buf[which, h] = (x_buf[which, :, columns(h)].astype(f32) + gates * picked).astype(bf16)

        @pl.when(section != (sections - 1) * (1 - which))
        def _():
            hand_over(which, h).start()

    def give(which, j, h, value):
        if j == 0:
            back_buf[which, h, 0] = value.astype(bf16)
        else:
            sz_buf[which, h, j] = value.astype(bf16)
            z_back(which, j, h).start()

    def w_start():
        w_copies[1].wait()
        for n in range(chunks):
            w_x(n).start()
        for n in range(chunks):
            w_core(n).start()

    def w_relay(n):
        w_x(n).wait_recv()
        w_far(n).start()

    def f_rows(j):
        z_out(0, j).wait_recv()

    def f_share(j):
        x_out(j).start()
        c_out(j).start()

    def f_relay(j):
        x_out(j).wait_recv()
        c_far(j).start()

    def f_hidden(j):
        await_bytes(rows_buf.at[j, pl.ds(1, 2)], c_sem.at[j])
        rows = rows_buf[j].reshape(SPLIT * cap, width)
        gate_up = jnp.dot(rows, win[...], preferred_element_type=f32)
        gate, up = gate_up[:, :hid], gate_up[:, hid:]
        hidden = (gate / (1.0 + jnp.exp(-gate)) * up).reshape(SPLIT, cap, hid).astype(bf16)
        h_buf[j, 0] = hidden[0]
        for mask in (3, 2, 1):
            h_send[j, mask] = hidden[mask]
            h_out(j, mask).start()

    def w_core_ready():
        await_bytes(wall.at[1], w_all_sem.at[0])

    def w_far_ready(c):
        await_bytes(wall.at[3, pl.ds(c * lot, lot)], w_all_sem.at[1 + c])

    def f_out(j):
        total = jnp.dot(h_buf[j, 0], wall[0].reshape(hid, width), preferred_element_type=f32)
        await_bytes(h_buf.at[j, pl.ds(1, SPLIT - 1)], hx_sem.at[j])
        for mask in range(1, SPLIT):
            total += jnp.dot(h_buf[j, mask], wall[mask].reshape(hid, width), preferred_element_type=f32)
        for h in range(HALVES):
            give(0, j, h, total[:, h * side : (h + 1) * side])

    def b_rows():
        await_bytes(z_buf.at[pl.ds(1, groups - 1)], zr_sem.at[0])

    def b_give(mask, c, grad):
        grad = grad.reshape(groups, cap, strip).astype(bf16)
        if mask:
            q_send[mask, c] = grad
            q_out(mask, c).start()
        else:
            q_buf[0, c] = grad

    def b_first(*masks):
        rows = z_buf[...].reshape(groups * cap, width)
        for mask in masks:
            grad = lax.dot_general(rows, wall[mask].reshape(hid, width), NT, preferred_element_type=f32)
            for c in range(lots):
                b_give(mask, c, grad[:, c * strip : (c + 1) * strip])

    def b_lot(mask, c):
        rows = z_buf[...].reshape(groups * cap, width)
        weights = wall[mask, pl.ds(c * lot, lot)].reshape(strip, width)
        b_give(mask, c, lax.dot_general(rows, weights, NT, preferred_element_type=f32))

    def b_ready():
        await_bytes(q_buf.at[pl.ds(1, SPLIT - 1)], qx_sem.at[0])
        await_bytes(stash_buf, stash_sem.at[0])

    def b_grad(j):
        saved = jnp.concatenate(
            [stash_buf[flipped(group, j), flipped(piece, mask)].astype(f32) for mask in range(SPLIT)], axis=0
        )
        grad = jnp.concatenate(
            [
                jnp.concatenate([q_buf[mask, c, j].astype(f32) for mask in range(SPLIT)], axis=0)
                for c in range(lots)
            ],
            axis=1,
        )
        gate, up = saved[:, :hid], saved[:, hid:]
        sig = 1.0 / (1.0 + jnp.exp(-gate))
        pre_buf[j] = jnp.concatenate(
            [grad * up * sig * (1.0 + gate * (1.0 - sig)), grad * gate * sig], axis=1
        ).astype(bf16)

    def b_part(j, h):
        part = lax.dot_general(pre_buf[j], win[columns(h)], NT, preferred_element_type=f32)
        part_buf[h, j] = part.reshape(SPLIT, cap, side).astype(bf16)
        r_far(j, h).start()
        r_own(j, h).start()

    def b_half(j, h):
        r_far(j, h).wait_recv()
        sx_buf[h, j] = (part_buf[h, j, 2].astype(f32) + red_far[h, j].astype(f32)).astype(bf16)
        r_x(j, h).start()

    def b_whole(j, h):
        await_bytes(red_buf.at[h, j], rw_sem.at[h, j])
        mine = part_buf[h, j, 0].astype(f32)
        give(1, j, h, mine + red_buf[h, j, 0].astype(f32) + red_buf[h, j, 1].astype(f32))

    outer = (group == 0) | (group == groups - 1)

    def outer_out(which):
        @pl.when(outer)
        def _():
            for j in order[half:-1] + order[:half]:
                z_out(which, j).start()

    def inner_out(which):
        @pl.when(jnp.logical_not(outer))
        def _():
            for j in order[:-1]:
                z_out(which, j).start()

    def begin(first):
        pack(first)
        ends = jnp.where(section == 0, 1, 0) + jnp.where(last, 1, 0)
        pl.semaphore_wait(barrier, groups + 5 - ends)
        w_start()
        outer_out(first)
        inner_out(first)
        pack(1 - first)
        outer_out(1 - first)
        for j in order:
            stash_copy(flipped(group, j)).start()
        w_copies[0].wait()
        for copy in small_copies[2:]:
            copy.wait()

    def settle(which):
        for kind, ref in (
            (Z_OUT, send_buf.at[:, pl.ds(1, groups - 1)]),
            (X_OUT, rows_buf.at[:, 0]),
            (C_OUT, rows_buf.at[:, 0]),
            (C_FAR, rows_buf.at[:, 2]),
            (W_X, wall.at[0]),
            (W_CORE, wall.at[0]),
            (W_FAR, wall.at[2]),
            (H_OUT, h_send.at[:, pl.ds(1, SPLIT - 1)]),
            (Q_OUT, q_send.at[pl.ds(1, SPLIT - 1)]),
            (R_OWN, part_buf.at[:, :, 1]),
            (R_FAR, part_buf.at[:, :, 3]),
            (R_X, sx_buf),
            (STASH, stash_buf),
        ):
            await_bytes(ref, sent.at[kind])
        settle_last(which)

    def settle_last(which):
        await_bytes(sz_buf.at[which, :, pl.ds(1, groups - 1)], sent.at[Z_BACK + which])

    far, mid = order[:half], order[half:-1]
    near = order[half:]

    @pl.when(section < sections - 1)
    def _():
        begin(0)
        for n in range(chunks // 2):
            w_relay(n)
        f_rows(far[0])
        f_share(far[0])
        for n in range(chunks // 2, chunks):
            w_relay(n)
            if n == chunks // 2:
                for j in far[1:]:
                    f_rows(j)
                    f_share(j)
                inner_out(1)
        w_core_ready()
        f_relay(far[0])
        for c in range(lots):
            w_far_ready(c)
        f_hidden(far[0])
        for j in mid:
            f_rows(j)
            f_share(j)
        for j in far[1:]:
            f_relay(j)
            f_hidden(j)
        f_share(0)
        f_out(far[0])
        b_rows()
        b_first(2, 3, 1, 0)
        for j in mid:
            f_relay(j)
        for j in far[1:]:
            f_out(j)
        for j in mid:
            f_hidden(j)
        f_relay(0)
        b_ready()
        for j in far[:1]:
            b_grad(j)
            b_part(j, 0)
            b_part(j, 1)
        f_hidden(0)
        for j in far[:1]:
            b_half(j, 0)
            b_half(j, 1)
        for j in mid:
            f_out(j)
        for j in far[1:]:
            b_grad(j)
            b_part(j, 0)
            b_part(j, 1)
            b_half(j, 0)
            b_half(j, 1)
        f_out(0)
        for j in mid:
            b_grad(j)
            b_part(j, 0)
            b_part(j, 1)
        b_whole(far[0], 0)
        for j in mid:
            b_half(j, 0)
        b_whole(far[0], 1)
        for j in mid:
            b_half(j, 1)
        b_grad(0)
        b_part(0, 0)
        b_part(0, 1)
        for j in far[1:]:
            b_whole(j, 0)
        b_half(0, 0)
        combine(0, 0)
        combine(0, 1)
        for j in far[1:]:
            b_whole(j, 1)
        b_half(0, 1)
        for j in mid:
            b_whole(j, 0)
            b_whole(j, 1)
        b_whole(0, 0)
        b_whole(0, 1)
        settle(0)
        combine(1, 0)
        combine(1, 1)
        settle_last(1)

    @pl.when(last)
    def _():
        begin(1)
        for n in range(lot):
            w_relay(n)
        b_rows()
        inner_out(0)
        for n in range(lot, chunks - 1):
            w_relay(n)
        for c in range(lots - 1):
            b_lot(2, c)
            w_far_ready(c)
            b_lot(3, c)
        w_core_ready()
        b_first(1, 0)
        for n in range(max(lot, chunks - 1), chunks):
            w_relay(n)
        b_lot(2, lots - 1)
        w_far_ready(lots - 1)
        b_lot(3, lots - 1)
        f_share(0)
        b_ready()
        b_grad(far[0])
        b_part(far[0], 0)
        b_part(far[0], 1)
        for j in far[1:]:
            b_grad(j)
        b_half(far[0], 0)
        for j in far[1:]:
            b_part(j, 0)
        b_half(far[0], 1)
        for j in far[1:]:
            b_part(j, 1)
        f_rows(far[0])
        f_share(far[0])
        for j in far[1:]:
            b_half(j, 0)
            b_half(j, 1)
        f_relay(0)
        for j in mid:
            b_grad(j)
            b_part(j, 0)
            b_part(j, 1)
        for j in mid:
            b_half(j, 0)
        b_whole(far[0], 0)
        b_whole(far[0], 1)
        f_relay(far[0])
        f_hidden(far[0])
        for j in mid:
            b_half(j, 1)
        for j in far[1:]:
            f_rows(j)
            f_share(j)
        b_grad(0)
        b_part(0, 0)
        b_part(0, 1)
        b_half(0, 0)
        for j in far[1:]:
            b_whole(j, 0)
        for j in mid:
            f_rows(j)
            f_share(j)
        for j in mid:
            b_whole(j, 0)
        for j in far[1:]:
            b_whole(j, 1)
        for j in mid:
            b_whole(j, 1)
        f_out(far[0])
        for j in far[1:]:
            f_relay(j)
            f_hidden(j)
        b_half(0, 1)
        b_whole(0, 0)
        combine(1, 0)
        f_hidden(0)
        for j in mid:
            f_relay(j)
        for j in far[1:]:
            f_out(j)
        for j in mid:
            f_hidden(j)
        b_whole(0, 1)
        combine(1, 1)
        for j in mid:
            f_out(j)
        f_out(0)
        settle(1)
        combine(0, 0)
        combine(0, 1)
        settle_last(0)

    for which in range(2):

        @pl.when(section != (sections - 1) * (1 - which))
        def _(which=which):
            await_bytes(y_buf.at[which], sent.at[HAND + which])

        @pl.when(section != (sections - 1) * which)
        def _(which=which):
            await_bytes((out_ref, grad_ref)[which], y_sem.at[which])


def place_kernel(sections, out_in, grad_in, out_ref, grad_ref, zeros, sem):
    section = lax.axis_index("section")

    def place(which, source):
        return pltpu.make_async_copy(source, (out_ref, grad_ref)[which], sem.at[which])

    for which, source in enumerate((out_in, grad_in)):

        @pl.when(section != (sections - 1) * which)
        def _(which=which, source=source):
            place(which, source).start()

        @pl.when(section == (sections - 1) * which)
        def _(which=which):
            zeros[...] = jnp.zeros(zeros.shape, zeros.dtype)
            place(which, zeros).start()

    for which in range(2):
        place(which, zeros).wait()


def solution(mesh):
    sections, shards = mesh.shape["section"], mesh.shape["expert"]
    groups = shards // SPLIT

    def per_device(fin, froute, fgate, cot, broute, bgate, stash, w_in, w_out):
        tokens, width = fin.shape[1:]
        rows, hid2 = stash.shape[2:]
        slots = rows // shards
        cap = -(-slots // 8) * 8
        hid = w_out.shape[2]
        saved = stash.reshape(shards, slots, hid2)
        if cap != slots:
            saved = jnp.pad(saved, ((0, 0), (0, cap - slots), (0, 0)))
        saved = saved.reshape(groups, SPLIT, cap, hid2)
        parts = next(n for n in (4, 3, 2, 1) if hid % (16 * n) == 0)
        lots = 2 if parts % 2 == 0 else 1
        bf16, dma = jnp.bfloat16, pltpu.SemaphoreType.DMA
        hbm = pl.BlockSpec(memory_space=pl.ANY)
        shape, held = jax.ShapeDtypeStruct((tokens, width), bf16), pltpu.VMEM((tokens, width), bf16)
        outputs, grads = pl.pallas_call(
            functools.partial(kernel, sections, groups),
            out_shape=(held, held),
            in_specs=[hbm] * 9,
            out_specs=(hbm, hbm),
            scratch_shapes=[
                pltpu.VMEM((2, 1, tokens), jnp.int32),
                pltpu.VMEM((2, 1, tokens), jnp.float32),
                pltpu.VMEM((2, tokens, width), bf16),
                pltpu.VMEM((2, HALVES, tokens, width // HALVES), bf16),
                pltpu.VMEM((2, groups * cap, tokens), bf16),
                pltpu.VMEM((2, groups, cap, width), bf16),
                pltpu.VMEM((groups, SPLIT, cap, width), bf16),
                pltpu.VMEM((groups, cap, width), bf16),
                pltpu.VMEM((groups, SPLIT, cap, hid), bf16),
                pltpu.VMEM((groups, SPLIT, cap, hid), bf16),
                pltpu.VMEM((SPLIT, lots, groups, cap, hid // lots), bf16),
                pltpu.VMEM((SPLIT, lots, groups, cap, hid // lots), bf16),
                pltpu.VMEM((groups, SPLIT * cap, hid2), bf16),
                pltpu.VMEM((HALVES, groups, SPLIT, cap, width // HALVES), bf16),
                pltpu.VMEM((HALVES, groups, 2, cap, width // HALVES), bf16),
                pltpu.VMEM((HALVES, groups, cap, width // HALVES), bf16),
                pltpu.VMEM((HALVES, groups, cap, width // HALVES), bf16),
                pltpu.VMEM((2, HALVES, groups, cap, width // HALVES), bf16),
                pltpu.VMEM((2, HALVES, groups, cap, width // HALVES), bf16),
                pltpu.VMEM((groups, SPLIT, cap, hid2), bf16),
                pltpu.VMEM((width, hid2), bf16),
                pltpu.VMEM((SPLIT, parts, hid // parts, width), bf16),
                dma((KINDS,)),
                dma((groups,)),
                dma((1,)),
                dma((groups,)),
                dma((groups,)),
                dma((parts,)),
                dma((1 + lots,)),
                dma((groups,)),
                dma((1,)),
                dma((HALVES, groups)),
                dma((HALVES, groups)),
                dma((2, HALVES)),
                dma((1,)),
                dma((2,)),
                dma((6,)),
                dma((2,)),
            ],
            compiler_params=pltpu.CompilerParams(
                collective_id=0, has_side_effects=True, vmem_limit_bytes=(64 * 1024 - 1280) * 1024
            ),
        )(
            fin[0],
            froute.reshape(1, tokens),
            fgate.reshape(1, tokens),
            cot[0],
            broute.reshape(1, tokens),
            bgate.reshape(1, tokens),
            saved,
            w_in[0, 0],
            w_out.reshape(parts, hid // parts, width),
        )
        outputs, grads = pl.pallas_call(
            functools.partial(place_kernel, sections),
            out_shape=(shape, shape),
            in_specs=[hbm, hbm],
            out_specs=(hbm, hbm),
            scratch_shapes=[pltpu.VMEM((tokens, width), bf16), dma((2,))],
            compiler_params=pltpu.CompilerParams(vmem_limit_bytes=8 * 1024 * 1024),
        )(outputs, grads)
        return outputs[None], grads[None]

    three, four = P("section", "expert", None), P("section", "expert", None, None)
    two = P("section", "expert")
    return jax.shard_map(
        per_device,
        mesh=mesh,
        in_specs=(three, three, two, three, three, two, four, four, four),
        out_specs=(three, three),
        check_vma=False,
    )
```

```python
import functools

import jax
import jax.numpy as jnp
from jax import lax
from jax.experimental import pallas as pl
from jax.experimental.pallas import tpu as pltpu
from jax.sharding import PartitionSpec as P

SPLIT, HALVES = 4, 2
MESH = pl.DeviceIdType.MESH
Z_OUT, X_OUT, C_OUT, C_FAR, W_X, W_CORE, W_FAR, H_OUT, Q_OUT, R_OWN, R_FAR, R_X, STASH, Z_BACK, HAND, KINDS = (
    *range(14),
    15,
    17,
)
NT = (((1,), (1,)), ((), ()))


def flipped(index, mask):
    bit = 1
    while bit <= mask:
        if mask & bit:
            index = index + bit - 2 * bit * ((index // bit) % 2)
        bit *= 2
    return index


def far_first(groups):
    half = groups // 2
    return sorted(range(1, groups), key=lambda j: (j < half, j)) + [0]


def kernel(
    sections,
    groups,
    fin_hbm,
    froute_hbm,
    fgate_hbm,
    cot_hbm,
    broute_hbm,
    bgate_hbm,
    stash_hbm,
    win_hbm,
    wout_hbm,
    out_ref,
    grad_ref,
    route_buf,
    gate_buf,
    x_buf,
    y_buf,
    place_buf,
    send_buf,
    rows_buf,
    z_buf,
    h_send,
    h_buf,
    q_send,
    q_buf,
    pre_buf,
    part_buf,
    red_buf,
    red_far,
    sx_buf,
    sz_buf,
    back_buf,
    stash_buf,
    win,
    wall,
    sent,
    zo_sem,
    zr_sem,
    xo_sem,
    c_sem,
    wx_sem,
    w_all_sem,
    hx_sem,
    qx_sem,
    rf_sem,
    rw_sem,
    zb_sem,
    stash_sem,
    y_sem,
    w_sem,
    x_sem,
):
    section = lax.axis_index("section")
    me = lax.axis_index("expert")
    group, piece = me // SPLIT, me % SPLIT
    tokens, width = x_buf.shape[1:]
    cap, side = send_buf.shape[2], width // HALVES
    chunks, hid = wall.shape[1], wall.shape[1] * wall.shape[2]
    lots = q_buf.shape[1]
    lot, strip = chunks // lots, hid // lots
    last = section == sections - 1
    mirror = sections - 1 - section
    order, half = far_first(groups), groups // 2
    bf16, f32 = jnp.bfloat16, jnp.float32

    def z_peer(j):
        return {"expert": flipped(group, j) * SPLIT + piece}

    def peer(mask):
        return {"expert": group * SPLIT + flipped(piece, mask)}

    def load(which):
        return pltpu.make_async_copy((fin_hbm, cot_hbm)[which], x_buf.at[which], x_sem.at[which])

    small_copies = [
        pltpu.make_async_copy(source, buf.at[which], w_sem.at[2 + n])
        for n, (source, buf, which) in enumerate(
            (
                (froute_hbm, route_buf, 0),
                (broute_hbm, route_buf, 1),
                (fgate_hbm, gate_buf, 0),
                (bgate_hbm, gate_buf, 1),
            )
        )
    ]
    for copy in small_copies:
        copy.start()
    load(0).start()
    load(1).start()
    barrier = pltpu.get_barrier_semaphore()

    def greet(where):
        pl.semaphore_signal(barrier, inc=1, device_id=where, device_id_type=MESH)

    for j in order[:-1]:
        greet(z_peer(j))
    for mask in range(1, SPLIT):
        greet(peer(mask))
    greet({"section": mirror})

    @pl.when(section < sections - 1)
    def _():
        greet({"section": section + 1})

    @pl.when(section > 0)
    def _():
        greet({"section": section - 1})

    def remote(src, dst, kind, landed, where):
        return pltpu.make_async_remote_copy(
            src_ref=src,
            dst_ref=dst,
            send_sem=sent.at[kind],
            recv_sem=landed,
            device_id=where,
            device_id_type=MESH,
        )

    def await_bytes(ref, semaphore):
        pltpu.make_async_copy(ref, ref, semaphore).wait()

    def z_out(which, j):
        if which:
            return remote(send_buf.at[1, j], z_buf.at[j], Z_OUT, zr_sem.at[0], z_peer(j))
        return remote(send_buf.at[0, j], rows_buf.at[j, 0], Z_OUT, zo_sem.at[j], z_peer(j))

    def x_out(j):
        return remote(rows_buf.at[j, 0], rows_buf.at[j, 2], X_OUT, xo_sem.at[j], peer(2))

    def c_out(j):
        return remote(rows_buf.at[j, 0], rows_buf.at[j, 1], C_OUT, c_sem.at[j], peer(1))

    def c_far(j):
        return remote(rows_buf.at[j, 2], rows_buf.at[j, 3], C_FAR, c_sem.at[j], peer(1))

    def w_x(n):
        return remote(wall.at[0, n], wall.at[2, n], W_X, wx_sem.at[n], peer(2))

    def w_core(n):
        return remote(wall.at[0, n], wall.at[1, n], W_CORE, w_all_sem.at[0], peer(1))

    def w_far(n):
        return remote(wall.at[2, n], wall.at[3, n], W_FAR, w_all_sem.at[1 + n // lot], peer(1))

    def h_out(j, mask):
        return remote(h_send.at[j, mask], h_buf.at[j, mask], H_OUT, hx_sem.at[j], peer(mask))

    def q_out(mask, c):
        return remote(q_send.at[mask, c], q_buf.at[mask, c], Q_OUT, qx_sem.at[0], peer(mask))

    def r_own(j, h):
        return remote(part_buf.at[h, j, 1], red_buf.at[h, j, 0], R_OWN, rw_sem.at[h, j], peer(1))

    def r_far(j, h):
        return remote(part_buf.at[h, j, 3], red_far.at[h, j], R_FAR, rf_sem.at[h, j], peer(1))

    def r_x(j, h):
        return remote(sx_buf.at[h, j], red_buf.at[h, j, 1], R_X, rw_sem.at[h, j], peer(2))

    def z_back(which, j, h):
        return remote(
            sz_buf.at[which, h, j], back_buf.at[which, h, j], Z_BACK + which, zb_sem.at[which, h], z_peer(j)
        )

    def stash_copy(n):
        return remote(stash_hbm.at[n], stash_buf.at[n], STASH, stash_sem.at[0], {"section": mirror})

    def columns(h):
        return pl.ds(h * side, side)

    def hand_over(which, h):
        return remote(
            y_buf.at[which, h],
            (out_ref, grad_ref)[which].at[:, columns(h)],
            HAND + which,
            y_sem.at[which],
            {"section": section + 1 - 2 * which},
        )

    w_copies = [pltpu.make_async_copy(win_hbm, win, w_sem.at[0])]
    w_copies.append(pltpu.make_async_copy(wout_hbm, wall.at[0], w_sem.at[1]))
    for copy in w_copies:
        copy.start()

    def pack(which):
        small_copies[which].wait()
        route = route_buf[which]
        lanes = max(8, groups)
        expert = lax.broadcasted_iota(jnp.int32, (lanes, tokens), 0)
        onehot = (expert == route).astype(f32)
        upper = lax.broadcasted_iota(jnp.int32, (tokens, tokens), 0) < lax.broadcasted_iota(
            jnp.int32, (tokens, tokens), 1
        )
        before = jnp.dot(onehot.astype(bf16), upper.astype(f32).astype(bf16), preferred_element_type=f32)
        rank = jnp.sum(before * onehot, axis=0, keepdims=True).astype(jnp.int32)
        position = jnp.bitwise_xor(route, group) * cap + rank
        slots = lax.broadcasted_iota(jnp.int32, (groups * cap, tokens), 0)
        place = (slots == position).astype(f32).astype(bf16)
        place_buf[which] = place
        load(which).wait()
        packed = jnp.dot(place, x_buf[which], preferred_element_type=f32)
        packed = packed.reshape(groups, cap, width).astype(bf16)
        for j in range(1, groups):
            send_buf[which, j] = packed[j]
        if which:
            z_buf[0] = packed[0]
        else:
            rows_buf[0, 0] = packed[0]

    def combine(which, h):
        eye = lax.broadcasted_iota(jnp.int32, (tokens, tokens), 0) == lax.broadcasted_iota(
            jnp.int32, (tokens, tokens), 1
        )
        gates = jnp.sum(jnp.where(eye, gate_buf[which], 0.0), axis=1, keepdims=True)
        await_bytes(back_buf.at[which, h, pl.ds(1, groups - 1)], zb_sem.at[which, h])
        picked = lax.dot_general(
            place_buf[which],
            back_buf[which, h].reshape(groups * cap, side),
            (((0,), (0,)), ((), ())),
            preferred_element_type=f32,
        )
        y_buf[which, h] = (x_buf[which, :, columns(h)].astype(f32) + gates * picked).astype(bf16)

        @pl.when(section != (sections - 1) * (1 - which))
        def _():
            hand_over(which, h).start()

    def give(which, j, h, value):
        if j == 0:
            back_buf[which, h, 0] = value.astype(bf16)
        else:
            sz_buf[which, h, j] = value.astype(bf16)
            z_back(which, j, h).start()

    def w_start():
        w_copies[1].wait()
        for n in range(chunks):
            w_x(n).start()
        for n in range(chunks):
            w_core(n).start()

    def w_relay(n):
        w_x(n).wait_recv()
        w_far(n).start()

    def f_rows(j):
        z_out(0, j).wait_recv()

    def f_share(j):
        x_out(j).start()
        c_out(j).start()

    def f_relay(j):
        x_out(j).wait_recv()
        c_far(j).start()

    def f_hidden(j):
        await_bytes(rows_buf.at[j, pl.ds(1, 2)], c_sem.at[j])
        rows = rows_buf[j].reshape(SPLIT * cap, width)
        gate_up = jnp.dot(rows, win[...], preferred_element_type=f32)
        gate, up = gate_up[:, :hid], gate_up[:, hid:]
        hidden = (gate / (1.0 + jnp.exp(-gate)) * up).reshape(SPLIT, cap, hid).astype(bf16)
        h_buf[j, 0] = hidden[0]
        for mask in (2, 3, 1):
            h_send[j, mask] = hidden[mask]
            h_out(j, mask).start()

    def w_core_ready():
        await_bytes(wall.at[1], w_all_sem.at[0])

    def w_far_ready(c):
        await_bytes(wall.at[3, pl.ds(c * lot, lot)], w_all_sem.at[1 + c])

    def f_out(j):
        total = jnp.dot(h_buf[j, 0], wall[0].reshape(hid, width), preferred_element_type=f32)
        await_bytes(h_buf.at[j, pl.ds(1, SPLIT - 1)], hx_sem.at[j])
        for mask in range(1, SPLIT):
            total += jnp.dot(h_buf[j, mask], wall[mask].reshape(hid, width), preferred_element_type=f32)
        for h in range(HALVES):
            give(0, j, h, total[:, h * side : (h + 1) * side])

    def b_rows():
        await_bytes(z_buf.at[pl.ds(1, groups - 1)], zr_sem.at[0])

    def b_give(mask, c, grad):
        grad = grad.reshape(groups, cap, strip).astype(bf16)
        if mask:
            q_send[mask, c] = grad
            q_out(mask, c).start()
        else:
            q_buf[0, c] = grad

    def b_first(*masks):
        rows = z_buf[...].reshape(groups * cap, width)
        for mask in masks:
            grad = lax.dot_general(rows, wall[mask].reshape(hid, width), NT, preferred_element_type=f32)
            for c in range(lots):
                b_give(mask, c, grad[:, c * strip : (c + 1) * strip])

    def b_lot(mask, c):
        rows = z_buf[...].reshape(groups * cap, width)
        weights = wall[mask, pl.ds(c * lot, lot)].reshape(strip, width)
        b_give(mask, c, lax.dot_general(rows, weights, NT, preferred_element_type=f32))

    def b_ready():
        await_bytes(q_buf.at[pl.ds(1, SPLIT - 1)], qx_sem.at[0])
        await_bytes(stash_buf, stash_sem.at[0])

    def b_grad(j):
        saved = jnp.concatenate(
            [stash_buf[flipped(group, j), flipped(piece, mask)].astype(f32) for mask in range(SPLIT)], axis=0
        )
        grad = jnp.concatenate(
            [
                jnp.concatenate([q_buf[mask, c, j].astype(f32) for mask in range(SPLIT)], axis=0)
                for c in range(lots)
            ],
            axis=1,
        )
        gate, up = saved[:, :hid], saved[:, hid:]
        sig = 1.0 / (1.0 + jnp.exp(-gate))
        pre_buf[j] = jnp.concatenate(
            [grad * up * sig * (1.0 + gate * (1.0 - sig)), grad * gate * sig], axis=1
        ).astype(bf16)

    def b_part(j, h):
        part = lax.dot_general(pre_buf[j], win[columns(h)], NT, preferred_element_type=f32)
        part_buf[h, j] = part.reshape(SPLIT, cap, side).astype(bf16)
        r_far(j, h).start()
        r_own(j, h).start()

    def b_half(j, h):
        r_far(j, h).wait_recv()
        sx_buf[h, j] = (part_buf[h, j, 2].astype(f32) + red_far[h, j].astype(f32)).astype(bf16)
        r_x(j, h).start()

    def b_whole(j, h):
        await_bytes(red_buf.at[h, j], rw_sem.at[h, j])
        mine = part_buf[h, j, 0].astype(f32)
        give(1, j, h, mine + red_buf[h, j, 0].astype(f32) + red_buf[h, j, 1].astype(f32))

    outer = (group == 0) | (group == groups - 1)

    def outer_out(which):
        @pl.when(outer)
        def _():
            for j in order[half:-1] + order[:half]:
                z_out(which, j).start()

    def inner_out(which):
        @pl.when(jnp.logical_not(outer))
        def _():
            for j in order[:-1]:
                z_out(which, j).start()

    def begin(first):
        pack(first)
        ends = jnp.where(section == 0, 1, 0) + jnp.where(last, 1, 0)
        pl.semaphore_wait(barrier, groups + 5 - ends)
        w_start()
        outer_out(first)
        inner_out(first)
        pack(1 - first)
        outer_out(1 - first)
        for j in order:
            stash_copy(flipped(group, j)).start()
        w_copies[0].wait()
        for copy in small_copies[2:]:
            copy.wait()

    def settle(which):
        for kind, ref in (
            (Z_OUT, send_buf.at[:, pl.ds(1, groups - 1)]),
            (X_OUT, rows_buf.at[:, 0]),
            (C_OUT, rows_buf.at[:, 0]),
            (C_FAR, rows_buf.at[:, 2]),
            (W_X, wall.at[0]),
            (W_CORE, wall.at[0]),
            (W_FAR, wall.at[2]),
            (H_OUT, h_send.at[:, pl.ds(1, SPLIT - 1)]),
            (Q_OUT, q_send.at[pl.ds(1, SPLIT - 1)]),
            (R_OWN, part_buf.at[:, :, 1]),
            (R_FAR, part_buf.at[:, :, 3]),
            (R_X, sx_buf),
            (STASH, stash_buf),
        ):
            await_bytes(ref, sent.at[kind])
        settle_last(which)

    def settle_last(which):
        await_bytes(sz_buf.at[which, :, pl.ds(1, groups - 1)], sent.at[Z_BACK + which])

    far, mid = order[:half], order[half:-1]
    near = order[half:]

    @pl.when(section < sections - 1)
    def _():
        begin(0)
        for n in range(chunks // 2):
            w_relay(n)
        f_rows(far[0])
        f_share(far[0])
        for n in range(chunks // 2, chunks):
            w_relay(n)
            if n == chunks // 2:
                for j in far[1:]:
                    f_rows(j)
                    f_share(j)
                inner_out(1)
        w_core_ready()
        f_relay(far[0])
        for c in range(lots):
            w_far_ready(c)
        f_hidden(far[0])
        for j in mid:
            f_rows(j)
            f_share(j)
        for j in far[1:]:
            f_relay(j)
            f_hidden(j)
        f_share(0)
        f_out(far[0])
        b_rows()
        b_first(2, 3, 1, 0)
        for j in mid:
            f_relay(j)
        for j in far[1:]:
            f_out(j)
        for j in mid:
            f_hidden(j)
        f_relay(0)
        b_ready()
        for j in far[:1]:
            b_grad(j)
            b_part(j, 0)
            b_part(j, 1)
        f_hidden(0)
        for j in far[:1]:
            b_half(j, 0)
            b_half(j, 1)
        for j in mid:
            f_out(j)
        for j in far[1:]:
            b_grad(j)
            b_part(j, 0)
            b_part(j, 1)
            b_half(j, 0)
            b_half(j, 1)
        f_out(0)
        for j in mid:
            b_grad(j)
            b_part(j, 0)
            b_part(j, 1)
        b_whole(far[0], 0)
        for j in mid:
            b_half(j, 0)
        b_whole(far[0], 1)
        for j in mid:
            b_half(j, 1)
        b_grad(0)
        b_part(0, 0)
        b_part(0, 1)
        for j in far[1:]:
            b_whole(j, 0)
        b_half(0, 0)
        combine(0, 0)
        combine(0, 1)
        for j in far[1:]:
            b_whole(j, 1)
        b_half(0, 1)
        for j in mid:
            b_whole(j, 0)
            b_whole(j, 1)
        b_whole(0, 0)
        b_whole(0, 1)
        settle(0)
        combine(1, 0)
        combine(1, 1)
        settle_last(1)

    @pl.when(last)
    def _():
        begin(1)
        for n in range(lot):
            w_relay(n)
        b_rows()
        inner_out(0)
        for n in range(lot, chunks - 1):
            w_relay(n)
        for c in range(lots - 1):
            b_lot(2, c)
            w_far_ready(c)
            b_lot(3, c)
        w_core_ready()
        b_first(1, 0)
        for n in range(max(lot, chunks - 1), chunks):
            w_relay(n)
        b_lot(2, lots - 1)
        w_far_ready(lots - 1)
        b_lot(3, lots - 1)
        f_share(0)
        b_ready()
        b_grad(far[0])
        b_part(far[0], 0)
        b_part(far[0], 1)
        for j in far[1:]:
            b_grad(j)
        b_half(far[0], 0)
        for j in far[1:]:
            b_part(j, 0)
        b_half(far[0], 1)
        for j in far[1:]:
            b_part(j, 1)
        f_rows(far[0])
        f_share(far[0])
        for j in far[1:]:
            b_half(j, 0)
            b_half(j, 1)
        f_relay(0)
        for j in mid:
            b_grad(j)
            b_part(j, 0)
            b_part(j, 1)
        for j in mid:
            b_half(j, 0)
        b_whole(far[0], 0)
        b_whole(far[0], 1)
        f_relay(far[0])
        f_hidden(far[0])
        for j in mid:
            b_half(j, 1)
        for j in far[1:]:
            f_rows(j)
            f_share(j)
        b_grad(0)
        b_part(0, 0)
        b_part(0, 1)
        b_half(0, 0)
        for j in far[1:]:
            b_whole(j, 0)
        for j in mid:
            f_rows(j)
            f_share(j)
        for j in mid:
            b_whole(j, 0)
        for j in far[1:]:
            b_whole(j, 1)
        for j in mid:
            b_whole(j, 1)
        f_out(far[0])
        for j in far[1:]:
            f_relay(j)
            f_hidden(j)
        b_half(0, 1)
        b_whole(0, 0)
        combine(1, 0)
        f_hidden(0)
        for j in mid:
            f_relay(j)
        for j in far[1:]:
            f_out(j)
        for j in mid:
            f_hidden(j)
        b_whole(0, 1)
        combine(1, 1)
        for j in mid:
            f_out(j)
        f_out(0)
        settle(1)
        combine(0, 0)
        combine(0, 1)
        settle_last(0)

    for which in range(2):

        @pl.when(section != (sections - 1) * (1 - which))
        def _(which=which):
            await_bytes(y_buf.at[which], sent.at[HAND + which])

        @pl.when(section != (sections - 1) * which)
        def _(which=which):
            await_bytes((out_ref, grad_ref)[which], y_sem.at[which])


def place_kernel(sections, out_in, grad_in, out_ref, grad_ref, zeros, sem):
    section = lax.axis_index("section")

    def place(which, source):
        return pltpu.make_async_copy(source, (out_ref, grad_ref)[which], sem.at[which])

    for which, source in enumerate((out_in, grad_in)):

        @pl.when(section != (sections - 1) * which)
        def _(which=which, source=source):
            place(which, source).start()

        @pl.when(section == (sections - 1) * which)
        def _(which=which):
            zeros[...] = jnp.zeros(zeros.shape, zeros.dtype)
            place(which, zeros).start()

    for which in range(2):
        place(which, zeros).wait()


def solution(mesh):
    sections, shards = mesh.shape["section"], mesh.shape["expert"]
    groups = shards // SPLIT

    def per_device(fin, froute, fgate, cot, broute, bgate, stash, w_in, w_out):
        tokens, width = fin.shape[1:]
        rows, hid2 = stash.shape[2:]
        slots = rows // shards
        cap = -(-slots // 8) * 8
        hid = w_out.shape[2]
        saved = stash.reshape(shards, slots, hid2)
        if cap != slots:
            saved = jnp.pad(saved, ((0, 0), (0, cap - slots), (0, 0)))
        saved = saved.reshape(groups, SPLIT, cap, hid2)
        parts = next(n for n in (6, 4, 3, 2, 1) if hid % (16 * n) == 0)
        lots = 2 if parts % 2 == 0 else 1
        bf16, dma = jnp.bfloat16, pltpu.SemaphoreType.DMA
        hbm = pl.BlockSpec(memory_space=pl.ANY)
        shape, held = jax.ShapeDtypeStruct((tokens, width), bf16), pltpu.VMEM((tokens, width), bf16)
        outputs, grads = pl.pallas_call(
            functools.partial(kernel, sections, groups),
            out_shape=(held, held),
            in_specs=[hbm] * 9,
            out_specs=(hbm, hbm),
            scratch_shapes=[
                pltpu.VMEM((2, 1, tokens), jnp.int32),
                pltpu.VMEM((2, 1, tokens), jnp.float32),
                pltpu.VMEM((2, tokens, width), bf16),
                pltpu.VMEM((2, HALVES, tokens, width // HALVES), bf16),
                pltpu.VMEM((2, groups * cap, tokens), bf16),
                pltpu.VMEM((2, groups, cap, width), bf16),
                pltpu.VMEM((groups, SPLIT, cap, width), bf16),
                pltpu.VMEM((groups, cap, width), bf16),
                pltpu.VMEM((groups, SPLIT, cap, hid), bf16),
                pltpu.VMEM((groups, SPLIT, cap, hid), bf16),
                pltpu.VMEM((SPLIT, lots, groups, cap, hid // lots), bf16),
                pltpu.VMEM((SPLIT, lots, groups, cap, hid // lots), bf16),
                pltpu.VMEM((groups, SPLIT * cap, hid2), bf16),
                pltpu.VMEM((HALVES, groups, SPLIT, cap, width // HALVES), bf16),
                pltpu.VMEM((HALVES, groups, 2, cap, width // HALVES), bf16),
                pltpu.VMEM((HALVES, groups, cap, width // HALVES), bf16),
                pltpu.VMEM((HALVES, groups, cap, width // HALVES), bf16),
                pltpu.VMEM((2, HALVES, groups, cap, width // HALVES), bf16),
                pltpu.VMEM((2, HALVES, groups, cap, width // HALVES), bf16),
                pltpu.VMEM((groups, SPLIT, cap, hid2), bf16),
                pltpu.VMEM((width, hid2), bf16),
                pltpu.VMEM((SPLIT, parts, hid // parts, width), bf16),
                dma((KINDS,)),
                dma((groups,)),
                dma((1,)),
                dma((groups,)),
                dma((groups,)),
                dma((parts,)),
                dma((1 + lots,)),
                dma((groups,)),
                dma((1,)),
                dma((HALVES, groups)),
                dma((HALVES, groups)),
                dma((2, HALVES)),
                dma((1,)),
                dma((2,)),
                dma((6,)),
                dma((2,)),
            ],
            compiler_params=pltpu.CompilerParams(
                collective_id=0, has_side_effects=True, vmem_limit_bytes=(64 * 1024 - 1280) * 1024
            ),
        )(
            fin[0],
            froute.reshape(1, tokens),
            fgate.reshape(1, tokens),
            cot[0],
            broute.reshape(1, tokens),
            bgate.reshape(1, tokens),
            saved,
            w_in[0, 0],
            w_out.reshape(parts, hid // parts, width),
        )
        outputs, grads = pl.pallas_call(
            functools.partial(place_kernel, sections),
            out_shape=(shape, shape),
            in_specs=[hbm, hbm],
            out_specs=(hbm, hbm),
            scratch_shapes=[pltpu.VMEM((tokens, width), bf16), dma((2,))],
            compiler_params=pltpu.CompilerParams(vmem_limit_bytes=8 * 1024 * 1024),
        )(outputs, grads)
        return outputs[None], grads[None]

    three, four = P("section", "expert", None), P("section", "expert", None, None)
    two = P("section", "expert")
    return jax.shard_map(
        per_device,
        mesh=mesh,
        in_specs=(three, three, two, three, three, two, four, four, four),
        out_specs=(three, three),
        check_vma=False,
    )
```
